128 devices in a mesh: blade: 32 (over z, y, core), span: 4 (over x).
Axes of the slice: x: 4, y: 4, z: 4, core: 2. Of those that a mesh axis runs over, the one named last changes fastest.
Arguments:
- solid_temp: float32 [8, 2048, 512], P(None, 'blade', 'span'), may hold values from 0.5 to 2.5
- base_conductivity: float32 [8, 2048, 512], P(None, 'blade', 'span'), may hold values from 0.3 to 3
- coolant_htc: float32 [2048, 512], P('blade', 'span'), may hold values from 0.3 to 3
- fluid_temp: float32 [262144], P(('blade', 'span')), may hold values from 1 to 3
- wall_htc: float32 [262144], P(('blade', 'span')), may hold values from 0.2 to 5
- face_dest: int32 [262144, 1], P(('blade', 'span')), may hold values from 0 to 127; in each aligned block of 2048 rows (0 to 2047, 2048 to 4095, ...) at most 32 rows name the same one
- face_cell: int32 [262144], P(('blade', 'span')), may hold values from 0 to 8191
- face_count: int32 [128], P(('blade', 'span')), may hold values from 1 to 2048, 196608 in all
Outputs:
- solid_out: float32 [8, 2048, 512], P(None, 'blade', 'span')
- fluid_out: float32 [262144], P(('blade', 'span'))
- wall_flux: float32 [262144], P(('blade', 'span'))
The draws below stay inside these ranges and needn't reach their ends.
Inputs may be any that keep to these rules, and one draw needn't show every extreme that they name: `face_dest`: among the 2048 slots of any one device no solid device is named by more than 32 slots, and some device's slots name one solid device exactly 32 times. `face_count`: some device has all 2048 slots live.
All inputs are finite; a program needn't handle non-finite values.
Results may differ from the reference program's by a relative error of at most 0.0003.
Values sent between devices are 32-bit elements; how exact they have to be, the bound alone decides.
A program may use at most 64 MiB of HBM per device.

```python
import math
import jax
import jax.numpy as jnp
import numpy as np

LAYERS = 8
CX = 64
CS = 128
FACE_SLOTS = 2048
SWEEPS = 6
SUBITERS = 4
NX = 2048
NS = 512
SURF = 8192
FACES = 262144
CAP = 32
N_SPAN = 4
DEVICES = 128


def plant(values, key, smallest, largest):
    index_at = [jax.random.randint(jax.random.fold_in(key, axis), (), 0, length) for axis, length in enumerate(values.shape)]
    longest = values.shape.index(max(values.shape))
    beside = index_at[:longest] + [(index_at[longest] + 1) % values.shape[longest]] + index_at[longest + 1:]
    return values.at[tuple(index_at)].set(smallest).at[tuple(beside)].set(largest)


def block_scale(key, extent, split, least, top_value):
    gain = 1.0
    for dim, blocks in split:
        heights = jax.random.uniform(jax.random.fold_in(jax.random.fold_in(key, 6), dim), (blocks,), jnp.float32, least / len(split), top_value / len(split))
        gain = gain * jnp.repeat(jnp.exp(heights), extent[dim] // blocks).reshape((-1,) + (1,) * (len(extent) - 1 - dim))
    return gain


def length_profile(count, total, reach, lean):
    loads = [(1 << 20) // math.isqrt(rank ** lean) + 1 for rank in range(2, count + 1)]
    spare, given = total - reach - (count - 1), [1] * (count - 1)
    while spare > 0:
        free = [i for i in range(count - 1) if given[i] < reach]
        whole, left = sum([loads[i] for i in free]), spare
        for i in free:
            extra = min(reach - given[i], max(1, left * loads[i] // whole), spare)
            given[i] = given[i] + extra
            spare = spare - extra
    return np.array([reach] + given)


def uneven_parts(rng, number_of, total, reach, slope):
    if number_of == 2:
        one = jax.random.randint(rng, (), max(1, total - reach), min(reach, total - 1) + 1)
        return jnp.stack([one, total - one])
    sizes = jnp.asarray(length_profile(number_of, total, reach, slope), jnp.int32)
    twos = (number_of - 1) // 2
    donor, sink = sizes[1:1 + 2 * twos:2], sizes[2:2 + 2 * twos:2]
    margin = jnp.minimum(donor - 1, reach - sink)
    moved = jax.random.randint(jax.random.fold_in(rng, 1), (twos,), 0, 1 << 20) % (margin + 1)
    sizes = sizes.at[1:1 + 2 * twos:2].set(donor - moved).at[2:2 + 2 * twos:2].set(sink + moved)
    return sizes[jax.random.permutation(jax.random.fold_in(rng, 2), number_of)]


def assign_block(stream_key, own, number, rows, amount, top, bound, lean):
    sequence = jax.random.permutation(stream_key, amount)
    packed, usual = shares(amount, rows * top, bound, lean, True), shares(amount, rows * top, bound, lean, False)
    places = jnp.arange(amount)

    def named(lengths, rotation):
        used = int((lengths > 0).sum())
        fixed = max(1, used // 4)
        moved = fixed + (places - fixed + rotation * (used - fixed)) % max(1, amount - fixed)
        return jnp.zeros((amount,), jnp.int32).at[sequence[jnp.where(places < fixed, places, moved)]].set(jnp.asarray(lengths, jnp.int32))

    lengths = jnp.where(number % 4 == 0, named(packed, number // 4), named(usual, number - number // 4 - 1))
    mixed = jax.random.permutation(jax.random.fold_in(own, 3), amount)
    giver, taker = mixed[0:amount // 2 * 2:2], mixed[1:amount // 2 * 2:2]
    slack = jnp.minimum(lengths[giver] - 1, bound - lengths[taker]) // 2
    slack = jnp.where((giver == sequence[0]) | (taker == sequence[0]) | (lengths[taker] == 0), 0, jnp.maximum(slack, 0))
    moved = jax.random.randint(jax.random.fold_in(own, 4), (amount // 2,), 0, 1 << 20) % (slack + 1)
    lengths = lengths.at[giver].add(-moved).at[taker].add(moved)
    labels = jnp.searchsorted(jnp.cumsum(lengths), jnp.arange(rows * top), side="right").astype(jnp.int32)
    grid = labels.reshape(top, rows).T
    grid = grid[jax.random.permutation(jax.random.fold_in(own, 1), rows)]
    rotation = jax.random.randint(jax.random.fold_in(own, 2), (rows, 1), 0, top)
    return jnp.take_along_axis(grid, (jnp.arange(top)[None, :] + rotation) % top, axis=1)


def shares(amount, total, bound, lean, full):
    portions = [(1 << 20) // math.isqrt(rank ** lean) + 1 for rank in range(1, amount + 1)]
    largest = bound if full else min(bound, max(-(-total // amount), total * portions[0] // sum(portions)))
    least = 1 if total - largest >= amount - 1 else 0
    given, surplus = [largest] + [least] * (amount - 1), total - largest - least * (amount - 1)
    while surplus > 0:
        free = [i for i in range(1, amount) if given[i] < largest] or [i for i in range(1, amount) if given[i] < bound]
        pool, budget = sum([portions[i] for i in free]), surplus
        for i in free:
            addition = min(bound - given[i], max(1, budget * portions[i] // pool), surplus)
            given[i] = given[i] + addition
            surplus = surplus - addition
    return np.array(given)


def setup_inputs(seed: int = 0) -> dict:
    splits = jax.random.split(jax.random.key(seed), 9)
    solid_temp = jnp.clip(0.5 + 2.0 * jax.random.uniform(splits[0], (LAYERS, NX, NS), jnp.float32) ** block_scale(splits[0], (LAYERS, NX, NS), ((1, 32), (2, 4)), -0.2, 0.2), 0.5, 2.5)
    base_conductivity = jnp.clip(jnp.exp(math.log(3.0) - 2.3025851 * jax.random.uniform(splits[1], (LAYERS, NX, NS), jnp.float32) ** block_scale(splits[1], (LAYERS, NX, NS), ((1, 32), (2, 4)), -0.2, 0.2)), 0.3, 3.0)
    coolant_htc = jnp.clip(jnp.exp(math.log(3.0) - 2.3025851 * jax.random.uniform(splits[2], (NX, NS), jnp.float32) ** block_scale(splits[2], (NX, NS), ((0, 32), (1, 4)), -0.2, 0.2)), 0.3, 3.0)
    fluid_temp = jnp.clip(1.0 + 2.0 * jax.random.uniform(splits[3], (FACES,), jnp.float32) ** block_scale(splits[3], (FACES,), ((0, 128),), -0.2, 0.2), 1.0, 3.0)
    wall_htc = jnp.clip(jnp.exp(math.log(5.0) - 3.218876 * jax.random.uniform(splits[4], (FACES,), jnp.float32) ** block_scale(splits[4], (FACES,), ((0, 128),), -0.2, 0.2)), 0.2, 5.0)
    face_dest_keys = jax.random.split(jax.random.fold_in(splits[5], 1), FACES // FACE_SLOTS)
    face_dest_turns = jax.random.permutation(jax.random.fold_in(splits[5], 3), FACES // FACE_SLOTS)
    face_dest = jax.vmap(lambda own, number: assign_block(jax.random.fold_in(splits[5], 2), own, number, FACE_SLOTS, DEVICES, 1, CAP, 2))(face_dest_keys, face_dest_turns).reshape((FACES, 1))
    face_cell = plant(jax.random.randint(splits[6], (FACES,), 0, SURF), jax.random.fold_in(splits[6], 1), 0, SURF - 1).astype(jnp.int32)
    face_count = uneven_parts(splits[7], DEVICES, 3 * FACES // 4, FACE_SLOTS, 2).astype(jnp.int32)
    return {"solid_temp": solid_temp, "base_conductivity": base_conductivity, "coolant_htc": coolant_htc, "fluid_temp": fluid_temp, "wall_htc": wall_htc, "face_dest": face_dest, "face_cell": face_cell, "face_count": face_count}


def shifted(arr, a, b, c):
    n0, n1, n2 = arr.shape
    return arr[1 + a:n0 - 1 + a, 1 + b:n1 - 1 + b, 1 + c:n2 - 1 + c]


def relax(padded_temp, padded_kappa, heat, heat_temp, coolant):
    cond = padded_kappa * (1.0 + 0.25 * padded_temp * padded_temp)
    centre = shifted(cond, 0, 0, 0)
    numer = jnp.zeros(centre.shape, jnp.float32)
    denom = jnp.zeros(centre.shape, jnp.float32)
    for a, b, c in ((1, 0, 0), (-1, 0, 0), (0, 1, 0), (0, -1, 0), (0, 0, 1), (0, 0, -1)):
        other = shifted(cond, a, b, c)
        weight = 2.0 * centre * other / (centre + other)
        numer = numer + weight * shifted(padded_temp, a, b, c)
        denom = denom + weight
    numer = numer.at[0].add(heat_temp)
    denom = denom.at[0].add(heat)
    denom = denom.at[-1].add(coolant)
    return numer / denom


def reference(solid_temp, base_conductivity, coolant_htc, fluid_temp, wall_htc, face_dest, face_cell, face_count):
    index = jnp.arange(FACES, dtype=jnp.int32)
    owner = index // FACE_SLOTS
    live = (index % FACE_SLOTS) < face_count[owner]
    dest = face_dest[:, 0]
    blade_idx = dest // N_SPAN
    span_idx = dest % N_SPAN
    row = (blade_idx * CX + face_cell // CS) * NS + span_idx * CS + face_cell % CS
    htc_live = jnp.where(live, wall_htc, 0.0)
    heat = jax.ops.segment_sum(htc_live, row, num_segments=NX * NS).reshape(NX, NS)
    kappa_pad = jnp.pad(base_conductivity, 1)
    temp = solid_temp
    tf = fluid_temp
    flux = jnp.zeros_like(fluid_temp)
    for outer in range(SUBITERS):
        heat_temp = jax.ops.segment_sum(htc_live * tf, row, num_segments=NX * NS).reshape(NX, NS)
        for inner in range(SWEEPS):
            temp = relax(jnp.pad(temp, 1), kappa_pad, heat, heat_temp, coolant_htc)
        wall = temp[0].reshape(-1)[row]
        q = wall_htc * (tf - wall)
        tf = jnp.where(live, tf - q / (wall_htc + 2.0), tf)
        flux = jnp.where(live, q, 0.0)
    return temp, tf, flux
```

```python
import functools

import jax
import jax.numpy as jnp
from jax import lax
from jax.experimental import pallas as pl
from jax.experimental.pallas import tpu as pltpu
from jax.sharding import PartitionSpec as P

SWEEPS = 6
SUBITERS = 4
HALO = SWEEPS * SUBITERS
LANES = 128
FIELDS = 2 * SUBITERS
CHUNK = 8
MESH = pl.DeviceIdType.MESH
f32 = jnp.float32
bf16 = jnp.bfloat16


def iota(shape, dim):
    return lax.broadcasted_iota(jnp.int32, shape, dim)


def split(value, parts):
    pieces = []
    for _ in range(parts):
        piece = value.astype(bf16)
        pieces.append(piece)
        value = value - piece.astype(f32)
    return pieces


def nt(a, b):
    return lax.dot_general(a, b, (((1,), (1,)), ((), ())), preferred_element_type=f32)


def nn(a, b):
    return jnp.dot(a, b, preferred_element_type=f32)


def kernel(
    n_blade,
    n_span,
    cap,
    solid_ref,
    kappa_ref,
    cool_ref,
    fluid_ref,
    htc_ref,
    dest_ref,
    cell_ref,
    count_ref,
    solid_out,
    fluid_out,
    flux_out,
    ext_t,
    ext_k,
    ext_c,
    ext_f,
    acc,
    temp_a,
    temp_b,
    kappa,
    cool,
    fields,
    numer_add,
    denom_add,
    tw,
    owner,
    rank,
    send_fwd,
    recv_fwd,
    send_back,
    recv_back,
    slot_x,
    slot_s,
    slot_v,
    pick_s,
    wall,
    local_sem,
    halo_send,
    halo_recv,
    face_send,
    face_recv,
):
    devices = n_blade * n_span
    layers, cells_x, cells_s = solid_ref.shape
    blocks = fluid_ref.shape[0]
    ib, js = lax.axis_index("blade"), lax.axis_index("span")
    me = ib * n_span + js
    lo, hi = HALO, HALO + cells_x
    rows = cells_s + 2 * HALO

    barrier = pltpu.get_barrier_semaphore()

    def place(k):
        peer = lax.rem(me + k, devices)
        return peer, (peer // n_span, lax.rem(peer, n_span))

    @pl.loop(1, devices)
    def _(k):
        _, at = place(k)
        pl.semaphore_signal(barrier, inc=1, device_id=at, device_id_type=MESH)

    inner_t = pltpu.make_async_copy(solid_ref, ext_t.at[:, lo:hi, :], local_sem.at[0])
    inner_k = pltpu.make_async_copy(kappa_ref, ext_k.at[:, lo:hi, :], local_sem.at[1])
    inner_t.start()
    inner_k.start()

    number = iota((blocks, LANES), 0) * LANES + iota((blocks, LANES), 1)
    live = number < jnp.broadcast_to(count_ref[...], (blocks, LANES))
    owner_row = jnp.where(live, dest_ref[...], -1)
    before = (iota((LANES, 2 * LANES), 0) < iota((LANES, 2 * LANES), 1)) | (
        iota((LANES, 2 * LANES), 1) >= LANES
    )
    before = before.astype(f32).astype(bf16)
    dev_iota = iota((LANES, LANES), 0)
    offset = jnp.zeros((LANES, LANES), f32)
    packed = jnp.zeros((LANES, LANES), f32)
    cell_f = cell_ref[...].astype(f32)
    slot_iota = iota((cap, LANES), 0).astype(f32)
    for b in range(blocks):
        mine = jnp.where(dev_iota == owner_row[b : b + 1, :], 1.0, 0.0)
        mine_b = mine.astype(bf16)
        owner[:, b * LANES : (b + 1) * LANES] = mine_b
        counts = nn(mine_b, before)
        order = jnp.sum(mine * (counts[:, :LANES] + offset), axis=0, keepdims=True)
        offset = offset + counts[:, LANES:]
        rank[b : b + 1, :] = order
        at_slot = slot_iota == order
        spread = jnp.concatenate(
            [
                jnp.where(at_slot, row[b : b + 1, :], 0.0)
                for row in (htc_ref[...], fluid_ref[...], cell_f)
            ]
            + [jnp.zeros((LANES - 3 * cap, LANES), f32)],
            axis=0,
        )
        for piece in split(spread, 3):
            packed = packed + nt(mine_b, piece)
    send_fwd[...] = packed.reshape(LANES, 1, LANES)
    if devices < LANES:
        recv_fwd[...] = jnp.zeros_like(recv_fwd)
        recv_back[...] = jnp.zeros_like(recv_back)

    pl.semaphore_wait(barrier, devices - 1)

    west = (lax.rem(ib + n_blade - 1, n_blade), js)
    east = (lax.rem(ib + 1, n_blade), js)
    south = (ib, lax.rem(js + n_span - 1, n_span))
    north = (ib, lax.rem(js + 1, n_span))

    def remote(src, dst, sem, to):
        return pltpu.make_async_remote_copy(
            src_ref=src,
            dst_ref=dst,
            send_sem=halo_send.at[sem],
            recv_sem=halo_recv.at[sem],
            device_id=to,
            device_id_type=MESH,
        )

    def across_blade(src, first, last, ext, sem):
        return (
            remote(src.at[..., first : first + HALO, :], ext.at[..., hi : hi + HALO, :], sem, west),
            remote(src.at[..., last - HALO : last, :], ext.at[..., 0:HALO, :], sem + 1, east),
        )

    x_halos = (
        across_blade(solid_ref, 0, cells_x, ext_t, 0)
        + across_blade(kappa_ref, 0, cells_x, ext_k, 2)
        + across_blade(cool_ref, 0, cells_x, ext_c, 4)
    )
    for copy in x_halos:
        copy.start()

    def exchange(send, recv, which):
        @pl.loop(1, devices)
        def _(k):
            peer, at = place(k)
            pltpu.make_async_remote_copy(
                src_ref=send.at[peer],
                dst_ref=recv.at[me],
                send_sem=face_send.at[which],
                recv_sem=face_recv.at[which],
                device_id=at,
                device_id_type=MESH,
            ).start()

        recv[pl.ds(me, 1)] = send[pl.ds(me, 1)]

    def arrived(send, recv, which):
        whole = pltpu.make_async_remote_copy(
            src_ref=send.at[pl.ds(0, devices - 1)],
            dst_ref=recv.at[pl.ds(0, devices - 1)],
            send_sem=face_send.at[which],
            recv_sem=face_recv.at[which],
            device_id=east,
            device_id_type=MESH,
        )
        whole.wait_send()
        whole.wait_recv()

    exchange(send_fwd, recv_fwd, 0)

    ext_c[lo:hi, :] = cool_ref[...]
    numer_add[...] = jnp.zeros_like(numer_add)
    denom_add[...] = jnp.zeros_like(denom_add)
    inner_t.wait()
    inner_k.wait()
    for copy in x_halos:
        copy.wait()
    for l in range(layers):
        temp_a[pl.ds(lo * 8 + l, cells_s, stride=8), :] = 0.5 * ext_t[l].T
        kappa[pl.ds(lo * 8 + l, cells_s, stride=8), :] = ext_k[l].T
    cool[lo : lo + cells_s, :] = ext_c[...].T

    def across_span(ref, unit, sem):
        first, last = lo * unit, (lo + cells_s) * unit
        width = HALO * unit

        def part(start):
            if len(ref.shape) == 3:
                return ref.at[:, start : start + width, :]
            return ref.at[start : start + width, :]

        return (
            remote(part(first), part(last), sem, south),
            remote(part(last - width), part(0), sem + 1, north),
        )

    s_halos = across_span(temp_a, 8, 6) + across_span(kappa, 8, 8) + across_span(cool, 1, 10)
    for copy in s_halos:
        copy.start()

    arrived(send_fwd, recv_fwd, 0)
    got = recv_fwd[...].reshape(LANES, LANES).T
    h = got[0:cap]
    tf = got[cap : 2 * cap]
    cell = got[2 * cap : 3 * cap].astype(jnp.int32)
    slot_x[...] = cell // cells_s
    slot_s[...] = cell % cells_s
    inv = 1.0 / (h + 2.0)
    keep = 2.0 * inv
    value = 0.5 * h
    slot_v[0] = value
    value = 0.25 * h * tf
    for n in range(SUBITERS):
        slot_v[1 + n] = value
        value = value * keep
    value = 0.5 * h * (h * inv)
    for n in range(SUBITERS - 1):
        slot_v[1 + SUBITERS + n] = value
        value = value * keep
    acc[...] = jnp.zeros_like(acc)
    x_iota = iota((cells_x, LANES), 0)
    s_iota = iota((cells_s, LANES), 0)

    group = 4

    @pl.loop(0, cap // group)
    def _(g):
        lhs, rhs = [], []
        for j in range(group):
            r = g * group + j
            row = pl.ds(r, 1)
            s_hit = jnp.where(s_iota == slot_s[row, :], 1.0, 0.0).astype(bf16)
            pick_s[:, pl.ds(pl.multiple_of(r * LANES, LANES), LANES)] = s_hit
            x_hit = x_iota == slot_x[row, :]
            upper, lower = [], []
            for k in range(FIELDS):
                v = slot_v[k, row, :]
                v_up = v.astype(bf16).astype(f32)
                upper.append(jnp.where(x_hit, v_up, 0.0).astype(bf16))
                lower.append(jnp.where(x_hit, v - v_up, 0.0).astype(bf16))
            lhs += [jnp.concatenate(upper, axis=0), jnp.concatenate(lower, axis=0)]
            rhs += [s_hit, s_hit]
        acc[...] += nt(jnp.concatenate(lhs, axis=1), jnp.concatenate(rhs, axis=1))

    for k in range(FIELDS):
        ext_f[k, lo:hi, :] = acc[k * cells_x : (k + 1) * cells_x, :]

    f_x = across_blade(ext_f, lo, hi, ext_f, 12)
    for copy in f_x:
        copy.start()

    for copy in s_halos:
        copy.wait()
    lane = iota((8, LANES), 1)
    inside_x = ((lane >= lo) | (ib > 0)) & ((lane < hi) | (ib < n_blade - 1))

    @pl.loop(0, rows)
    def _(s):
        inside = inside_x & (((s >= lo) | (js > 0)) & ((s < lo + cells_s) | (js < n_span - 1)))
        at = pl.ds(pl.multiple_of(s * 8, 8), 8)
        kappa[at, :] = jnp.where(inside, kappa[at, :], 1e-15)

    for copy in f_x:
        copy.wait()
    for k in range(FIELDS):
        fields[k, lo : lo + cells_s, :] = ext_f[k].T
    f_s = across_span(fields, 1, 14)
    for copy in f_s:
        copy.start()
    for copy in f_s:
        copy.wait()

    every = pl.ds(0, rows, stride=8)
    denom_add[every, :] = fields[0]
    denom_add[pl.ds(layers - 1, rows, stride=8), :] = 0.5 * cool[...]
    not_last = jnp.where(iota((8, LANES), 0) < layers - 1, 1.0, 0.0)

    def conduct(t, k):
        return k + k * (t * t)

    def weight(a, b):
        return a * b / (a + b)

    def sweep(src, dst, step):
        first = step + 1

        def tile(ref, s):
            return ref[pl.ds(pl.multiple_of(s * 8, 8), 8), :]

        def chunk(i, carry):
            t_prev, t_here, c_here, w_prev = carry
            for j in range(CHUNK):
                s = first + i * CHUNK + j
                t_next = tile(src, s + 1)
                c_next = conduct(t_next, tile(kappa, s + 1))
                w_next = weight(c_here, c_next)
                w_up = weight(c_here, pltpu.roll(c_here, LANES - 1, 1))
                w_down = pltpu.roll(w_up, 1, 1)
                w_in = weight(c_here, pltpu.roll(c_here, 7, 0)) * not_last
                w_out = pltpu.roll(w_in, 1, 0)
                numer = (
                    (w_next * t_next + w_prev * t_prev)
                    + (w_up * pltpu.roll(t_here, LANES - 1, 1) + w_down * pltpu.roll(t_here, 1, 1))
                    + (w_in * pltpu.roll(t_here, 7, 0) + w_out * pltpu.roll(t_here, 1, 0))
                    + tile(numer_add, s)
                )
                denom = ((w_next + w_prev) + (w_up + w_down)) + (
                    (w_in + w_out) + tile(denom_add, s)
                )
                dst[pl.ds(pl.multiple_of(s * 8, 8), 8), :] = numer / denom
                t_prev, t_here, c_here, w_prev = t_here, t_next, c_next, w_next
            return t_prev, t_here, c_here, w_prev

        t_prev, t_here = tile(src, first - 1), tile(src, first)
        c_prev = conduct(t_prev, tile(kappa, first - 1))
        c_here = conduct(t_here, tile(kappa, first))
        count = (rows - 2 * first + CHUNK - 1) // CHUNK
        lax.fori_loop(0, count, chunk, (t_prev, t_here, c_here, weight(c_prev, c_here)))

    for n in range(SUBITERS):
        extra = fields[1 + n]
        for m in range(n):
            extra = extra + tw[m] * fields[SUBITERS + n - m]
        numer_add[every, :] = extra

        @pl.loop(0, SWEEPS // 2)
        def _(p):
            step = n * SWEEPS + 2 * p
            sweep(temp_a, temp_b, step)
            sweep(temp_b, temp_a, step + 1)

        now = temp_a[every, :]
        tw[n] = now
        rows_x = now[lo : lo + cells_s, :].T[lo:hi, :]
        up, low = split(rows_x, 2)
        wall[2 * n * cells_x : (2 * n + 1) * cells_x, :] = up
        wall[(2 * n + 1) * cells_x : (2 * n + 2) * cells_x, :] = low

    @pl.loop(0, cap)
    def _(r):
        row = pl.ds(r, 1)
        lanes = pl.ds(pl.multiple_of(r * LANES, LANES), LANES)
        found = nn(wall[...], pick_s[:, lanes])
        x_hit = x_iota == slot_x[row, :]
        for n in range(SUBITERS):
            both = (
                found[2 * n * cells_x : (2 * n + 1) * cells_x]
                + found[(2 * n + 1) * cells_x : (2 * n + 2) * cells_x]
            )
            slot_v[n, row, :] = jnp.sum(jnp.where(x_hit, both, 0.0), axis=0, keepdims=True)

    got = recv_fwd[...].reshape(LANES, LANES).T
    h = got[0:cap]
    tf = got[cap : 2 * cap]
    inv = 1.0 / (h + 2.0)
    for n in range(SUBITERS):
        q = h * (tf - 2.0 * slot_v[n])
        tf = tf - q * inv
    back = jnp.concatenate([q, tf, jnp.zeros((LANES - 2 * cap, LANES), f32)], axis=0)
    send_back[...] = back.T.reshape(LANES, 1, LANES)
    exchange(send_back, recv_back, 1)

    for l in range(layers):
        final = temp_a[pl.ds(lo * 8 + l, cells_s, stride=8), :]
        solid_out[l] = 2.0 * final.T[lo:hi, :]

    arrived(send_back, recv_back, 1)
    table = recv_back[...].reshape(LANES, LANES).T[0 : 2 * cap]
    pieces = jnp.concatenate(split(table, 3), axis=0)
    for b in range(blocks):
        seen = nn(pieces, owner[:, b * LANES : (b + 1) * LANES])
        seen = seen[0 : 2 * cap] + seen[2 * cap : 4 * cap] + seen[4 * cap : 6 * cap]
        at_slot = slot_iota == rank[b : b + 1, :]
        q_row = jnp.sum(jnp.where(at_slot, seen[0:cap], 0.0), axis=0, keepdims=True)
        t_row = jnp.sum(jnp.where(at_slot, seen[cap : 2 * cap], 0.0), axis=0, keepdims=True)
        on = live[b : b + 1, :]
        flux_out[b : b + 1, :] = jnp.where(on, q_row, 0.0)
        fluid_out[b : b + 1, :] = jnp.where(on, t_row, fluid_ref[b : b + 1, :])


def shards(
    n_blade,
    n_span,
    solid_temp,
    base_conductivity,
    coolant_htc,
    fluid_temp,
    wall_htc,
    face_dest,
    face_cell,
    face_count,
):
    layers, cells_x, cells_s = solid_temp.shape
    slots = fluid_temp.shape[0]
    cap = 32
    blocks = slots // LANES
    rows = cells_s + 2 * HALO
    tall = rows + CHUNK
    vmem = pl.BlockSpec(memory_space=pltpu.VMEM)
    hbm = pl.BlockSpec(memory_space=pl.ANY)
    big = pltpu.VMEM((tall * 8, LANES), f32)
    faces = pltpu.VMEM((LANES, 1, LANES), f32)
    ext = pltpu.VMEM((layers, LANES, cells_s), f32)
    temp, fluid, flux = pl.pallas_call(
        functools.partial(kernel, n_blade, n_span, cap),
        out_shape=(
            jax.ShapeDtypeStruct(solid_temp.shape, f32),
            jax.ShapeDtypeStruct((blocks, LANES), f32),
            jax.ShapeDtypeStruct((blocks, LANES), f32),
        ),
        in_specs=[hbm, hbm, vmem, vmem, vmem, vmem, vmem, vmem],
        out_specs=(vmem, vmem, vmem),
        scratch_shapes=[
            ext,
            ext,
            pltpu.VMEM((LANES, cells_s), f32),
            ext,
            pltpu.VMEM((FIELDS * cells_x, cells_s), f32),
            big,
            big,
            big,
            pltpu.VMEM((rows, LANES), f32),
            pltpu.VMEM((FIELDS, rows, LANES), f32),
            big,
            big,
            pltpu.VMEM((SUBITERS, rows, LANES), f32),
            pltpu.VMEM((LANES, slots), bf16),
            pltpu.VMEM((blocks, LANES), f32),
            faces,
            faces,
            faces,
            faces,
            pltpu.VMEM((cap, LANES), jnp.int32),
            pltpu.VMEM((cap, LANES), jnp.int32),
            pltpu.VMEM((FIELDS, cap, LANES), f32),
            pltpu.VMEM((cells_s, cap * LANES), bf16),
            pltpu.VMEM((2 * SUBITERS * cells_x, cells_s), bf16),
            pltpu.SemaphoreType.DMA((2,)),
            pltpu.SemaphoreType.DMA((16,)),
            pltpu.SemaphoreType.DMA((16,)),
            pltpu.SemaphoreType.DMA((2,)),
            pltpu.SemaphoreType.DMA((2,)),
        ],
        compiler_params=pltpu.CompilerParams(
            collective_id=0, has_side_effects=True, vmem_limit_bytes=48 << 20
        ),
    )(
        solid_temp,
        base_conductivity,
        coolant_htc,
        fluid_temp.reshape(blocks, LANES),
        wall_htc.reshape(blocks, LANES),
        face_dest.reshape(blocks, LANES),
        face_cell.reshape(blocks, LANES),
        face_count.reshape(1, 1),
    )
    return temp, fluid.reshape(slots), flux.reshape(slots)


def solution(mesh):
    placed = (
        P(None, "blade", "span"),
        P(None, "blade", "span"),
        P("blade", "span"),
        P(("blade", "span")),
        P(("blade", "span")),
        P(("blade", "span"), None),
        P(("blade", "span")),
        P(("blade", "span")),
    )
    return jax.shard_map(
        functools.partial(shards, mesh.shape["blade"], mesh.shape["span"]),
        mesh=mesh,
        in_specs=placed,
        out_specs=(P(None, "blade", "span"), P(("blade", "span")), P(("blade", "span"))),
        check_vma=False,
    )
```

```python
import functools

import jax
import jax.numpy as jnp
from jax import lax
from jax.experimental import pallas as pl
from jax.experimental.pallas import tpu as pltpu
from jax.sharding import PartitionSpec as P

SWEEPS = 6
SUBITERS = 4
HALO = SWEEPS * SUBITERS
LANES = 128
FIELDS = 2 * SUBITERS
PIECES = 3
CHUNK = 16
PAD = 16
MESH = pl.DeviceIdType.MESH
f32 = jnp.float32
bf16 = jnp.bfloat16


def iota(shape, dim):
    return lax.broadcasted_iota(jnp.int32, shape, dim)


def split(value, parts):
    pieces = []
    for _ in range(parts):
        piece = value.astype(bf16)
        pieces.append(piece)
        value = value - piece.astype(f32)
    return pieces


def nt(a, b):
    return lax.dot_general(a, b, (((1,), (1,)), ((), ())), preferred_element_type=f32)


def nn(a, b):
    return jnp.dot(a, b, preferred_element_type=f32)


def kernel(
    n_blade,
    n_span,
    cap,
    solid_ref,
    kappa_ref,
    cool_ref,
    fluid_ref,
    htc_ref,
    dest_ref,
    cell_ref,
    count_ref,
    solid_out,
    fluid_out,
    flux_out,
    fluid,
    htc,
    dest,
    cells,
    ext_t,
    ext_k,
    ext_c,
    ext_f,
    acc,
    state_a,
    state_b,
    rho,
    rho_up,
    rho_down,
    cool,
    fields,
    numer_add,
    denom_add,
    tw,
    owner,
    rank,
    send_fwd,
    recv_fwd,
    send_back,
    recv_back,
    slot_x,
    slot_s,
    slot_v,
    pick,
    wall,
    local_sem,
    halo_send,
    halo_recv,
    face_send,
    face_recv,
):
    devices = n_blade * n_span
    layers, cells_x, cells_s = solid_ref.shape
    blocks = fluid_ref.shape[0]
    temp_a = state_a[0]
    ib, js = lax.axis_index("blade"), lax.axis_index("span")
    me = ib * n_span + js
    lo, hi = HALO, HALO + cells_x
    rows = cells_s + 2 * HALO

    barrier = pltpu.get_barrier_semaphore()

    loads = [
        pltpu.make_async_copy(src, dst, local_sem.at[i])
        for i, (src, dst) in enumerate(
            (
                (dest_ref, dest),
                (cell_ref, cells),
                (htc_ref, htc),
                (fluid_ref, fluid),
                (solid_ref, ext_t.at[:, lo:hi, :]),
                (kappa_ref, ext_k.at[:, lo:hi, :]),
                (cool_ref, ext_c.at[lo:hi, :]),
            )
        )
    ]
    for load in loads:
        load.start()

    def peers(visit):
        unit = 7 if (devices - 1) % 7 == 1 else 1
        if unit > 1:
            visit_one(visit, devices - 1)

        @pl.loop(0, (devices - 1) // unit)
        def _(i):
            for j in range(unit):
                visit_one(visit, i * unit + j + 1)

    def visit_one(visit, k):
        peer = lax.rem(me + k, devices)
        visit(peer, (lax.div(peer, n_span), lax.rem(peer, n_span)))

    peers(
        lambda _, at: pl.semaphore_signal(barrier, inc=1, device_id=at, device_id_type=MESH)
    )
    for load in loads[:4]:
        load.wait()

    number = iota((blocks, LANES), 0) * LANES + iota((blocks, LANES), 1)
    live = number < jnp.broadcast_to(count_ref[...], (blocks, LANES))
    owner_row = jnp.where(live, dest[...], -1)
    before = (iota((LANES, 2 * LANES), 0) < iota((LANES, 2 * LANES), 1)) | (
        iota((LANES, 2 * LANES), 1) >= LANES
    )
    before = before.astype(f32).astype(bf16)
    dev_iota = iota((LANES, LANES), 0)
    offset = jnp.zeros((LANES, LANES), f32)
    packed = jnp.zeros((LANES, LANES), f32)
    cell_f = cells[...].astype(f32)
    slot_iota = iota((cap, LANES), 0).astype(f32)
    for b in range(blocks):
        mine = jnp.where(dev_iota == owner_row[b : b + 1, :], 1.0, 0.0)
        mine_b = mine.astype(bf16)
        owner[:, b * LANES : (b + 1) * LANES] = mine_b
        counts = nn(mine_b, before)
        order = jnp.sum(mine * (counts[:, :LANES] + offset), axis=0, keepdims=True)
        offset = offset + counts[:, LANES:]
        rank[b : b + 1, :] = order
        at_slot = slot_iota == order
        spread = jnp.concatenate(
            [
                jnp.where(at_slot, row[b : b + 1, :], 0.0)
                for row in (htc[...], fluid[...], cell_f)
            ]
            + [jnp.zeros((LANES - 3 * cap, LANES), f32)],
            axis=0,
        )
        for piece in split(spread, 3):
            packed = packed + nt(mine_b, piece)
    send_fwd[...] = packed.reshape(LANES, 1, LANES)
    if devices < LANES:
        recv_fwd[...] = jnp.zeros_like(recv_fwd)
        recv_back[...] = jnp.zeros_like(recv_back)

    pl.semaphore_wait(barrier, devices - 1)

    west = (lax.rem(ib + n_blade - 1, n_blade), js)
    east = (lax.rem(ib + 1, n_blade), js)
    south = (ib, lax.rem(js + n_span - 1, n_span))
    north = (ib, lax.rem(js + 1, n_span))

    def remote(src, dst, sem, to):
        return pltpu.make_async_remote_copy(
            src_ref=src,
            dst_ref=dst,
            send_sem=halo_send.at[sem],
            recv_sem=halo_recv.at[sem],
            device_id=to,
            device_id_type=MESH,
        )

    def across_blade(src, first, last, ext, sem):
        return (
            remote(src.at[..., first : first + HALO, :], ext.at[..., hi : hi + HALO, :], sem, west),
            remote(src.at[..., last - HALO : last, :], ext.at[..., 0:HALO, :], sem + 1, east),
        )

    x_halos = (
        across_blade(solid_ref, 0, cells_x, ext_t, 0)
        + across_blade(kappa_ref, 0, cells_x, ext_k, 2)
        + across_blade(cool_ref, 0, cells_x, ext_c, 4)
    )
    for copy in x_halos:
        copy.start()

    def exchange(send, recv, which):
        peers(
            lambda peer, at: pltpu.make_async_remote_copy(
                src_ref=send.at[peer],
                dst_ref=recv.at[me],
                send_sem=face_send.at[which],
                recv_sem=face_recv.at[which],
                device_id=at,
                device_id_type=MESH,
            ).start()
        )

        recv[pl.ds(me, 1)] = send[pl.ds(me, 1)]

    def arrived(send, recv, which):
        whole = pltpu.make_async_remote_copy(
            src_ref=send.at[pl.ds(0, devices - 1)],
            dst_ref=recv.at[pl.ds(0, devices - 1)],
            send_sem=face_send.at[which],
            recv_sem=face_recv.at[which],
            device_id=east,
            device_id_type=MESH,
        )
        whole.wait_send()
        whole.wait_recv()

    exchange(send_fwd, recv_fwd, 0)

    numer_add[...] = jnp.zeros_like(numer_add)
    denom_add[...] = jnp.zeros_like(denom_add)
    for load in loads[4:]:
        load.wait()
    for copy in x_halos:
        copy.wait()
    for l in range(layers):
        column = pl.ds((PAD + lo) * 8 + l, cells_s, stride=8)
        temp_a[column, :] = 0.5 * ext_t[l].T
        rho[column, :] = 1.0 / ext_k[l].T
    cool[lo : lo + cells_s, :] = ext_c[...].T

    def across_span(ref, unit, pad, sem):
        first, last = (pad + lo) * unit, (pad + lo + cells_s) * unit
        width = HALO * unit

        def part(start):
            if len(ref.shape) == 3:
                return ref.at[:, start : start + width, :]
            return ref.at[start : start + width, :]

        return (
            remote(part(first), part(last), sem, south),
            remote(part(last - width), part(pad * unit), sem + 1, north),
        )

    s_halos = (
        across_span(temp_a, 8, PAD, 6)
        + across_span(rho, 8, PAD, 8)
        + across_span(cool, 1, 0, 10)
    )
    for copy in s_halos:
        copy.start()

    arrived(send_fwd, recv_fwd, 0)
    got = recv_fwd[...].reshape(LANES, LANES).T
    h = got[0:cap]
    tf = got[cap : 2 * cap]
    cell = got[2 * cap : 3 * cap].astype(jnp.int32)
    x_cell = cell // cells_s
    slot_x[...] = x_cell // 2
    slot_s[...] = cell - (x_cell // 2) * (2 * cells_s)
    inv = 1.0 / (h + 2.0)
    keep = 2.0 * inv
    value = 0.5 * h
    slot_v[0] = value
    value = 0.25 * h * tf
    for n in range(SUBITERS):
        slot_v[1 + n] = value
        value = value * keep
    value = 0.5 * h * (h * inv)
    for n in range(SUBITERS - 1):
        slot_v[1 + SUBITERS + n] = value
        value = value * keep
    acc[...] = jnp.zeros_like(acc)
    half = cells_x // 2
    x_iota = iota((half, LANES), 0)
    s_iota = iota((2 * cells_s, LANES), 0)
    group = 4

    @pl.loop(0, cap // group)
    def _(g):
        lhs, rhs = [], []
        for j in range(group):
            r = g * group + j
            row = pl.ds(r, 1)
            s_hit = jnp.where(s_iota == slot_s[row, :], 1.0, 0.0).astype(bf16)
            pick[:, pl.ds(pl.multiple_of(r * LANES, LANES), LANES)] = s_hit
            x_hit = x_iota == slot_x[row, :]
            upper, lower = [], []
            for k in range(FIELDS):
                v = slot_v[k, row, :]
                v_up = v.astype(bf16).astype(f32)
                upper.append(jnp.where(x_hit, v_up, 0.0).astype(bf16))
                lower.append(jnp.where(x_hit, v - v_up, 0.0).astype(bf16))
            lhs += [jnp.concatenate(upper, axis=0), jnp.concatenate(lower, axis=0)]
            rhs += [s_hit, s_hit]
        acc[...] += nt(jnp.concatenate(lhs, axis=1), jnp.concatenate(rhs, axis=1))

    for k in range(FIELDS):
        for odd in range(2):
            ext_f[k, pl.ds(lo + odd, half, stride=2), :] = acc[
                k * half : (k + 1) * half, odd * cells_s : (odd + 1) * cells_s
            ]

    f_x = across_blade(ext_f, lo, hi, ext_f, 12)
    for copy in f_x:
        copy.start()

    for copy in s_halos:
        copy.wait()
    lane = iota((8, LANES), 1)
    inside_x = ((lane >= lo) | (ib > 0)) & ((lane < hi) | (ib < n_blade - 1))

    def tile(s):
        return pl.ds(pl.multiple_of((s + PAD) * 8, 8), 8)

    def sides(s, to, count=CHUNK):
        for j in range(count):
            at = tile(s + j)
            t = to[0][at, :]
            to[1][at, :] = pltpu.roll(t, LANES - 1, 1)
            to[2][at, :] = pltpu.roll(t, 1, 1)

    @pl.loop(0, rows // 8)
    def _(i):
        inside = inside_x & (
            ((i >= lo // 8) | (js > 0)) & ((i < (lo + cells_s) // 8) | (js < n_span - 1))
        )
        for j in range(8):
            at = tile(i * 8 + j)
            held = jnp.where(inside, rho[at, :], 1e15)
            rho[at, :] = held
            rho_up[at, :] = pltpu.roll(held, LANES - 1, 1)
            rho_down[at, :] = pltpu.roll(held, 1, 1)
        sides(i * 8, state_a, 8)

    for copy in f_x:
        copy.wait()
    for k in range(FIELDS):
        fields[k, lo : lo + cells_s, :] = ext_f[k].T
    f_s = across_span(fields, 1, 0, 14)
    for copy in f_s:
        copy.start()
    for copy in f_s:
        copy.wait()

    every = pl.ds(PAD * 8, rows, stride=8)
    denom_add[every, :] = fields[0]
    denom_add[pl.ds(PAD * 8 + layers - 1, rows, stride=8), :] = 0.5 * cool[...]
    not_last = jnp.where(iota((8, LANES), 0) < layers - 1, 1.0, 0.0)

    def sweep(src, dst, step):
        first = step + 1

        def chunk(i, carry):
            t_prev, t_here, r_here, w_prev = carry
            start = first + i * CHUNK
            sides(start - CHUNK, dst)
            for j in range(CHUNK):
                at, after = tile(start + j), tile(start + j + 1)
                t_next = src[0][after, :]
                r_next = resist(t_next, rho[after, :])
                t_up, t_down = src[1][at, :], src[2][at, :]
                w_next = 1.0 / (r_here + r_next)
                w_up = 1.0 / (r_here + resist(t_up, rho_up[at, :]))
                w_down = 1.0 / (r_here + resist(t_down, rho_down[at, :]))
                w_in = not_last / (r_here + pltpu.roll(r_here, 7, 0))
                w_out = pltpu.roll(w_in, 1, 0)
                numer = (
                    (w_next * t_next + w_prev * t_prev)
                    + (w_up * t_up + w_down * t_down)
                    + (w_in * pltpu.roll(t_here, 7, 0) + w_out * pltpu.roll(t_here, 1, 0))
                    + numer_add[at, :]
                )
                denom = ((w_next + w_prev) + (w_up + w_down)) + (
                    (w_in + w_out) + denom_add[at, :]
                )
                dst[0][at, :] = numer / denom
                t_prev, t_here, r_here, w_prev = t_here, t_next, r_next, w_next
            return t_prev, t_here, r_here, w_prev

        def resist(t, held):
            return held / (1.0 + t * t)

        before, here = tile(first - 1), tile(first)
        t_prev, t_here = src[0][before, :], src[0][here, :]
        r_here = resist(t_here, rho[here, :])
        w_prev = 1.0 / (resist(t_prev, rho[before, :]) + r_here)
        count = (rows - 2 * first + CHUNK - 1) // CHUNK
        lax.fori_loop(0, count, chunk, (t_prev, t_here, r_here, w_prev))
        sides(first + (count - 1) * CHUNK, dst)

    for n in range(SUBITERS):
        extra = fields[1 + n]
        for m in range(n):
            extra = extra + tw[m] * fields[SUBITERS + n - m]
        numer_add[every, :] = extra

        @pl.loop(0, SWEEPS // 2)
        def _(p):
            step = n * SWEEPS + 2 * p
            sweep(state_a, state_b, step)
            sweep(state_b, state_a, step + 1)

        now = temp_a[every, :]
        tw[n] = now
        wall_x = now[lo : lo + cells_s, :].T
        ext_c[...] = wall_x
        for odd in range(2):
            pieces = split(ext_c[pl.ds(lo + odd, half, stride=2), :], PIECES)
            for p, piece in enumerate(pieces):
                at = (n * PIECES + p) * half
                wall[at : at + half, odd * cells_s : (odd + 1) * cells_s] = piece

    @pl.loop(0, cap // 2)
    def _(g):
        lanes = pl.ds(pl.multiple_of(g * 2 * LANES, 2 * LANES), 2 * LANES)
        found = nn(wall[...], pick[:, lanes])
        for j in range(2):
            row = pl.ds(g * 2 + j, 1)
            x_hit = x_iota == slot_x[row, :]
            for n in range(SUBITERS):
                at = n * PIECES * half
                total = found[at : at + half, j * LANES : (j + 1) * LANES]
                for p in range(1, PIECES):
                    total = total + found[
                        at + p * half : at + (p + 1) * half, j * LANES : (j + 1) * LANES
                    ]
                slot_v[n, row, :] = jnp.sum(jnp.where(x_hit, total, 0.0), axis=0, keepdims=True)

    got = recv_fwd[...].reshape(LANES, LANES).T
    h = got[0:cap]
    tf = got[cap : 2 * cap]
    inv = 1.0 / (h + 2.0)
    for n in range(SUBITERS):
        q = h * (tf - 2.0 * slot_v[n])
        tf = tf - q * inv
    back = jnp.concatenate([q, tf, jnp.zeros((LANES - 2 * cap, LANES), f32)], axis=0)
    send_back[...] = back.T.reshape(LANES, 1, LANES)
    exchange(send_back, recv_back, 1)

    for l in range(layers):
        final = temp_a[pl.ds((PAD + lo) * 8 + l, cells_s, stride=8), :]
        solid_out[l] = 2.0 * final.T[lo:hi, :]

    arrived(send_back, recv_back, 1)
    table = recv_back[...].reshape(LANES, LANES).T[0 : 2 * cap]
    pieces = jnp.concatenate(split(table, 3), axis=0)
    for b in range(blocks):
        seen = nn(pieces, owner[:, b * LANES : (b + 1) * LANES])
        seen = seen[0 : 2 * cap] + seen[2 * cap : 4 * cap] + seen[4 * cap : 6 * cap]
        at_slot = slot_iota == rank[b : b + 1, :]
        q_row = jnp.sum(jnp.where(at_slot, seen[0:cap], 0.0), axis=0, keepdims=True)
        t_row = jnp.sum(jnp.where(at_slot, seen[cap : 2 * cap], 0.0), axis=0, keepdims=True)
        on = live[b : b + 1, :]
        flux_out[b : b + 1, :] = jnp.where(on, q_row, 0.0)
        fluid_out[b : b + 1, :] = jnp.where(on, t_row, fluid[b : b + 1, :])


def shards(
    n_blade,
    n_span,
    solid_temp,
    base_conductivity,
    coolant_htc,
    fluid_temp,
    wall_htc,
    face_dest,
    face_cell,
    face_count,
):
    layers, cells_x, cells_s = solid_temp.shape
    slots = fluid_temp.shape[0]
    cap = 32
    blocks = slots // LANES
    rows = cells_s + 2 * HALO
    tall = rows + 2 * PAD
    vmem = pl.BlockSpec(memory_space=pltpu.VMEM)
    hbm = pl.BlockSpec(memory_space=pltpu.HBM)
    big = pltpu.VMEM((tall * 8, LANES), f32)
    faces_f = pltpu.VMEM((blocks, LANES), f32)
    faces_i = pltpu.VMEM((blocks, LANES), jnp.int32)
    faces = pltpu.VMEM((LANES, 1, LANES), f32)
    ext = pltpu.VMEM((layers, LANES, cells_s), f32)
    temp, fluid, flux = pl.pallas_call(
        functools.partial(kernel, n_blade, n_span, cap),
        out_shape=(
            jax.ShapeDtypeStruct(solid_temp.shape, f32),
            jax.ShapeDtypeStruct((blocks, LANES), f32),
            jax.ShapeDtypeStruct((blocks, LANES), f32),
        ),
        in_specs=[hbm] * 7 + [vmem],
        out_specs=(vmem, vmem, vmem),
        scratch_shapes=[
            faces_f,
            faces_f,
            faces_i,
            faces_i,
            ext,
            ext,
            pltpu.VMEM((LANES, cells_s), f32),
            ext,
            pltpu.VMEM((FIELDS * cells_x // 2, 2 * cells_s), f32),
            [big] * 3,
            [big] * 3,
            big,
            big,
            big,
            pltpu.VMEM((rows, LANES), f32),
            pltpu.VMEM((FIELDS, rows, LANES), f32),
            big,
            big,
            pltpu.VMEM((SUBITERS, rows, LANES), f32),
            pltpu.VMEM((LANES, slots), bf16),
            pltpu.VMEM((blocks, LANES), f32),
            faces,
            faces,
            faces,
            faces,
            pltpu.VMEM((cap, LANES), jnp.int32),
            pltpu.VMEM((cap, LANES), jnp.int32),
            pltpu.VMEM((FIELDS, cap, LANES), f32),
            pltpu.VMEM((2 * cells_s, cap * LANES), bf16),
            pltpu.VMEM((SUBITERS * PIECES * cells_x // 2, 2 * cells_s), bf16),
            pltpu.SemaphoreType.DMA((7,)),
            pltpu.SemaphoreType.DMA((16,)),
            pltpu.SemaphoreType.DMA((16,)),
            pltpu.SemaphoreType.DMA((2,)),
            pltpu.SemaphoreType.DMA((2,)),
        ],
        compiler_params=pltpu.CompilerParams(
            collective_id=0, has_side_effects=True, vmem_limit_bytes=48 << 20
        ),
    )(
        solid_temp,
        base_conductivity,
        coolant_htc,
        fluid_temp.reshape(blocks, LANES),
        wall_htc.reshape(blocks, LANES),
        face_dest.reshape(blocks, LANES),
        face_cell.reshape(blocks, LANES),
        face_count.reshape(1, 1),
    )
    return temp, fluid.reshape(slots), flux.reshape(slots)


def solution(mesh):
    placed = (
        P(None, "blade", "span"),
        P(None, "blade", "span"),
        P("blade", "span"),
        P(("blade", "span")),
        P(("blade", "span")),
        P(("blade", "span"), None),
        P(("blade", "span")),
        P(("blade", "span")),
    )
    return jax.shard_map(
        functools.partial(shards, mesh.shape["blade"], mesh.shape["span"]),
        mesh=mesh,
        in_specs=placed,
        out_specs=(P(None, "blade", "span"), P(("blade", "span")), P(("blade", "span"))),
        check_vma=False,
    )
```

```python
import functools

import jax
import jax.numpy as jnp
from jax import lax
from jax.experimental import pallas as pl
from jax.experimental.pallas import tpu as pltpu
from jax.sharding import PartitionSpec as P

SWEEPS = 6
SUBITERS = 4
HALO = SWEEPS * SUBITERS
LANES = 128
FIELDS = 2 * SUBITERS
PIECES = 3
CHUNK = 16
PAD = 16
SPAN_HALO = HALO // 2
EDGE = 16
MESH = pl.DeviceIdType.MESH
f32 = jnp.float32
bf16 = jnp.bfloat16


def iota(shape, dim):
    return lax.broadcasted_iota(jnp.int32, shape, dim)


def split(value, parts):
    pieces = []
    for _ in range(parts):
        piece = value.astype(bf16)
        pieces.append(piece)
        value = value - piece.astype(f32)
    return pieces


def nt(a, b):
    return lax.dot_general(a, b, (((1,), (1,)), ((), ())), preferred_element_type=f32)


def nn(a, b):
    return jnp.dot(a, b, preferred_element_type=f32)


def kernel(
    n_blade,
    n_span,
    cap,
    solid_ref,
    kappa_ref,
    cool_ref,
    fluid_ref,
    htc_ref,
    dest_ref,
    cell_ref,
    count_ref,
    solid_out,
    fluid_out,
    flux_out,
    fluid,
    htc,
    dest,
    cells,
    ext_t,
    ext_k,
    ext_c,
    ext_f,
    acc,
    state_a,
    state_b,
    rho,
    rho_up,
    rho_down,
    cool,
    fields,
    numer_add,
    denom_add,
    tw,
    owner,
    rank,
    send_fwd,
    recv_fwd,
    send_back,
    recv_back,
    slot_x,
    slot_s,
    slot_v,
    pick,
    wall,
    local_sem,
    halo_send,
    halo_recv,
    face_send,
    face_recv,
    landing,
    landing_tw,
):
    devices = n_blade * n_span
    layers, cells_x, cells_s = solid_ref.shape
    blocks = fluid_ref.shape[0]
    temp_a = state_a[0]
    ib, js = lax.axis_index("blade"), lax.axis_index("span")
    me = ib * n_span + js
    lo, hi = HALO, HALO + cells_x
    s_lo, s_hi = EDGE, EDGE + cells_s
    rows = cells_s + 2 * EDGE

    barrier = pltpu.get_barrier_semaphore()

    loads = [
        pltpu.make_async_copy(src, dst, local_sem.at[i])
        for i, (src, dst) in enumerate(
            (
                (dest_ref, dest),
                (cell_ref, cells),
                (htc_ref, htc),
                (fluid_ref, fluid),
                (solid_ref, ext_t.at[:, lo:hi, :]),
                (kappa_ref, ext_k.at[:, lo:hi, :]),
                (cool_ref, ext_c.at[lo:hi, :]),
            )
        )
    ]
    for load in loads:
        load.start()

    def peers(visit):
        unit = 7 if (devices - 1) % 7 == 1 else 1
        if unit > 1:
            visit_one(visit, devices - 1)

        @pl.loop(0, (devices - 1) // unit)
        def _(i):
            for j in range(unit):
                visit_one(visit, i * unit + j + 1)

    def visit_one(visit, k):
        peer = lax.rem(me + k, devices)
        visit(peer, (lax.div(peer, n_span), lax.rem(peer, n_span)))

    peers(
        lambda _, at: pl.semaphore_signal(barrier, inc=1, device_id=at, device_id_type=MESH)
    )
    for load in loads[:4]:
        load.wait()

    number = iota((blocks, LANES), 0) * LANES + iota((blocks, LANES), 1)
    live = number < jnp.broadcast_to(count_ref[...], (blocks, LANES))
    owner_row = jnp.where(live, dest[...], -1)
    before = (iota((LANES, 2 * LANES), 0) < iota((LANES, 2 * LANES), 1)) | (
        iota((LANES, 2 * LANES), 1) >= LANES
    )
    before = before.astype(f32).astype(bf16)
    dev_iota = iota((LANES, LANES), 0)
    offset = jnp.zeros((LANES, LANES), f32)
    packed = jnp.zeros((LANES, LANES), f32)
    cell_f = cells[...].astype(f32)
    slot_iota = iota((cap, LANES), 0).astype(f32)
    for b in range(blocks):
        mine = jnp.where(dev_iota == owner_row[b : b + 1, :], 1.0, 0.0)
        mine_b = mine.astype(bf16)
        owner[:, b * LANES : (b + 1) * LANES] = mine_b
        counts = nn(mine_b, before)
        order = jnp.sum(mine * (counts[:, :LANES] + offset), axis=0, keepdims=True)
        offset = offset + counts[:, LANES:]
        rank[b : b + 1, :] = order
        at_slot = slot_iota == order
        spread = jnp.concatenate(
            [
                jnp.where(at_slot, row[b : b + 1, :], 0.0)
                for row in (htc[...], fluid[...], cell_f)
            ]
            + [jnp.zeros((LANES - 3 * cap, LANES), f32)],
            axis=0,
        )
        for piece in split(spread, 3):
            packed = packed + nt(mine_b, piece)
    send_fwd[...] = packed.reshape(LANES, 1, LANES)
    if devices < LANES:
        recv_fwd[...] = jnp.zeros_like(recv_fwd)
        recv_back[...] = jnp.zeros_like(recv_back)

    pl.semaphore_wait(barrier, devices - 1)

    west = (lax.rem(ib + n_blade - 1, n_blade), js)
    east = (lax.rem(ib + 1, n_blade), js)
    south = (ib, lax.rem(js + n_span - 1, n_span))
    north = (ib, lax.rem(js + 1, n_span))

    def remote(src, dst, sem, to):
        return pltpu.make_async_remote_copy(
            src_ref=src,
            dst_ref=dst,
            send_sem=halo_send.at[sem],
            recv_sem=halo_recv.at[sem],
            device_id=to,
            device_id_type=MESH,
        )

    def across_blade(src, first, last, ext, sem):
        return (
            remote(src.at[..., first : first + HALO, :], ext.at[..., hi : hi + HALO, :], sem, west),
            remote(src.at[..., last - HALO : last, :], ext.at[..., 0:HALO, :], sem + 1, east),
        )

    x_halos = (
        across_blade(solid_ref, 0, cells_x, ext_t, 0)
        + across_blade(kappa_ref, 0, cells_x, ext_k, 2)
        + across_blade(cool_ref, 0, cells_x, ext_c, 4)
    )
    for copy in x_halos:
        copy.start()

    def exchange(send, recv, which):
        peers(
            lambda peer, at: pltpu.make_async_remote_copy(
                src_ref=send.at[peer],
                dst_ref=recv.at[me],
                send_sem=face_send.at[which],
                recv_sem=face_recv.at[which],
                device_id=at,
                device_id_type=MESH,
            ).start()
        )

        recv[pl.ds(me, 1)] = send[pl.ds(me, 1)]

    def arrived(send, recv, which):
        whole = pltpu.make_async_remote_copy(
            src_ref=send.at[pl.ds(0, devices - 1)],
            dst_ref=recv.at[pl.ds(0, devices - 1)],
            send_sem=face_send.at[which],
            recv_sem=face_recv.at[which],
            device_id=east,
            device_id_type=MESH,
        )
        whole.wait_send()
        whole.wait_recv()

    exchange(send_fwd, recv_fwd, 0)

    numer_add[...] = jnp.zeros_like(numer_add)
    denom_add[...] = jnp.zeros_like(denom_add)
    for load in loads[4:]:
        load.wait()
    for copy in x_halos:
        copy.wait()
    for l in range(layers):
        column = pl.ds((PAD + s_lo) * 8 + l, cells_s, stride=8)
        temp_a[column, :] = 0.5 * ext_t[l].T
        rho[column, :] = 1.0 / ext_k[l].T
    cool[s_lo:s_hi, :] = ext_c[...].T

    def across_span(ref, unit, pad, count, sem, land=None):
        first, last = (pad + s_lo) * unit, (pad + s_hi) * unit
        width = count * unit

        def part(start):
            if len(ref.shape) == 3:
                return ref.at[:, start : start + width, :]
            return ref.at[start : start + width, :]

        above, below = (part(last), part(first - width)) if land is None else land
        return (
            remote(part(first), above, sem, south),
            remote(part(last - width), below, sem + 1, north),
        )

    s_halos = (
        across_span(temp_a, 8, PAD, SPAN_HALO, 6)
        + across_span(rho, 8, PAD, SPAN_HALO, 8)
        + across_span(cool, 1, 0, EDGE, 10)
    )
    for copy in s_halos:
        copy.start()

    arrived(send_fwd, recv_fwd, 0)
    got = recv_fwd[...].reshape(LANES, LANES).T
    h = got[0:cap]
    tf = got[cap : 2 * cap]
    cell = got[2 * cap : 3 * cap].astype(jnp.int32)
    x_cell = cell // cells_s
    slot_x[...] = x_cell // 2
    slot_s[...] = cell - (x_cell // 2) * (2 * cells_s)
    inv = 1.0 / (h + 2.0)
    keep = 2.0 * inv
    value = 0.5 * h
    slot_v[0] = value
    value = 0.25 * h * tf
    for n in range(SUBITERS):
        slot_v[1 + n] = value
        value = value * keep
    value = 0.5 * h * (h * inv)
    for n in range(SUBITERS - 1):
        slot_v[1 + SUBITERS + n] = value
        value = value * keep
    acc[...] = jnp.zeros_like(acc)
    half = cells_x // 2
    x_iota = iota((half, LANES), 0)
    s_iota = iota((2 * cells_s, LANES), 0)
    group = 4

    def scatter(fresh, chosen):
        span = 2 * len(chosen) * half
        base = 2 * chosen[0] * half

        @pl.loop(0, cap // group)
        def _(g):
            lhs, rhs = [], []
            for j in range(group):
                r = g * group + j
                row = pl.ds(r, 1)
                lanes = pl.ds(pl.multiple_of(r * LANES, LANES), LANES)
                if fresh:
                    s_hit = jnp.where(s_iota == slot_s[row, :], 1.0, 0.0).astype(bf16)
                    pick[:, lanes] = s_hit
                else:
                    s_hit = pick[:, lanes]
                x_hit = x_iota == slot_x[row, :]
                upper, lower = [], []
                for k in chosen:
                    v = slot_v[k, row, :]
                    v_up = v.astype(bf16).astype(f32)
                    upper.append(jnp.where(x_hit, v_up, 0.0).astype(bf16))
                    lower.append(jnp.where(x_hit, v - v_up, 0.0).astype(bf16))
                lhs.append(jnp.concatenate(upper + lower, axis=0))
                rhs.append(s_hit)
            acc[base : base + span, :] += nt(
                jnp.concatenate(lhs, axis=1), jnp.concatenate(rhs, axis=1)
            )

        for i, k in enumerate(chosen):
            for odd in range(2):
                lanes = slice(odd * cells_s, (odd + 1) * cells_s)
                up = base + i * half
                low = up + len(chosen) * half
                ext_f[k, pl.ds(lo + odd, half, stride=2), :] = (
                    acc[up : up + half, lanes] + acc[low : low + half, lanes]
                )

    def turn(chosen):
        for k in chosen:
            fields[k, s_lo:s_hi, :] = ext_f[k].T

    soon, later = range(0, 2), range(2, FIELDS)
    ext_soon, ext_later = ext_f.at[0:2], ext_f.at[2:FIELDS]
    scatter(True, soon)
    f_x = across_blade(ext_soon, lo, hi, ext_soon, 12)
    for copy in f_x:
        copy.start()
    scatter(False, later)
    late_x = across_blade(ext_later, lo, hi, ext_later, 18)
    for copy in late_x:
        copy.start()

    lane = iota((8, LANES), 1)
    inside_x = ((lane >= lo) | (ib > 0)) & ((lane < hi) | (ib < n_blade - 1))

    def tile(s):
        return pl.ds(pl.multiple_of((s + PAD) * 8, 8), 8)

    def sides(s, to, count=CHUNK):
        for j in range(count):
            at = tile(s + j)
            t = to[0][at, :]
            to[1][at, :] = pltpu.roll(t, LANES - 1, 1)
            to[2][at, :] = pltpu.roll(t, 1, 1)

    def fill(i):
        inside = inside_x & (
            ((i >= s_lo // 8) | (js > 0)) & ((i < s_hi // 8) | (js < n_span - 1))
        )
        for j in range(8):
            at = tile(i * 8 + j)
            held = jnp.where(inside, rho[at, :], 1e15)
            rho[at, :] = held
            rho_up[at, :] = pltpu.roll(held, LANES - 1, 1)
            rho_down[at, :] = pltpu.roll(held, 1, 1)
        sides(i * 8, state_a, 8)

    edge = EDGE // 8

    @pl.loop(2 * edge, rows // 8 - 2 * edge)
    def _(i):
        fill(i)

    for copy in f_x:
        copy.wait()
    turn(soon)
    f_s = across_span(fields.at[0:2], 1, 0, EDGE, 14)
    for copy in f_s:
        copy.start()
    for copy in s_halos:
        copy.wait()

    @pl.loop(0, 2 * edge)
    def _(i):
        fill(i)
        fill(i + rows // 8 - 2 * edge)

    for copy in late_x:
        copy.wait()
    turn(later)
    late_s = across_span(fields.at[2:FIELDS], 1, 0, EDGE, 20)
    for copy in late_s:
        copy.start()
    for copy in f_s:
        copy.wait()

    every = pl.ds(PAD * 8, rows, stride=8)
    denom_add[every, :] = fields[0]
    denom_add[pl.ds(PAD * 8 + layers - 1, rows, stride=8), :] = 0.5 * cool[...]
    not_last = jnp.where(iota((8, LANES), 0) < layers - 1, 1.0, 0.0)

    def sweep(src, dst, step):
        first = EDGE - SPAN_HALO + 1 + step

        def chunk(i, carry):
            t_prev, t_here, r_here, w_prev = carry
            start = first + i * CHUNK
            sides(start - CHUNK, dst)
            for j in range(CHUNK):
                at, after = tile(start + j), tile(start + j + 1)
                t_next = src[0][after, :]
                r_next = resist(t_next, rho[after, :])
                t_up, t_down = src[1][at, :], src[2][at, :]
                w_next = 1.0 / (r_here + r_next)
                w_up = 1.0 / (r_here + resist(t_up, rho_up[at, :]))
                w_down = 1.0 / (r_here + resist(t_down, rho_down[at, :]))
                w_in = not_last / (r_here + pltpu.roll(r_here, 7, 0))
                w_out = pltpu.roll(w_in, 1, 0)
                numer = (
                    (w_next * t_next + w_prev * t_prev)
                    + (w_up * t_up + w_down * t_down)
                    + (w_in * pltpu.roll(t_here, 7, 0) + w_out * pltpu.roll(t_here, 1, 0))
                    + numer_add[at, :]
                )
                denom = ((w_next + w_prev) + (w_up + w_down)) + (
                    (w_in + w_out) + denom_add[at, :]
                )
                dst[0][at, :] = numer / denom
                t_prev, t_here, r_here, w_prev = t_here, t_next, r_next, w_next
            return t_prev, t_here, r_here, w_prev

        def resist(t, held):
            return held / (1.0 + t * t)

        before, here = tile(first - 1), tile(first)
        t_prev, t_here = src[0][before, :], src[0][here, :]
        r_here = resist(t_here, rho[here, :])
        w_prev = 1.0 / (resist(t_prev, rho[before, :]) + r_here)
        count = (rows - 2 * first + CHUNK - 1) // CHUNK
        lax.fori_loop(0, count, chunk, (t_prev, t_here, r_here, w_prev))
        sides(first + (count - 1) * CHUNK, dst)

    def find(early):
        pair = 2 * PIECES * half

        @pl.loop(0, cap // group)
        def _(g):
            width = group * LANES
            lanes = pl.ds(pl.multiple_of(g * width, width), width)
            found = nn(wall[early * PIECES * half : early * PIECES * half + pair, :], pick[:, lanes])
            for j in range(group):
                row = pl.ds(g * group + j, 1)
                x_hit = x_iota == slot_x[row, :]
                for n in range(2):
                    at = n * PIECES * half
                    total = found[at : at + half, j * LANES : (j + 1) * LANES]
                    for p in range(1, PIECES):
                        total = total + found[
                            at + p * half : at + (p + 1) * half, j * LANES : (j + 1) * LANES
                        ]
                    slot_v[early + n, row, :] = jnp.sum(
                        jnp.where(x_hit, total, 0.0), axis=0, keepdims=True
                    )

    for n in range(SUBITERS):
        if n == 1:
            for copy in late_s:
                copy.wait()
        extra = fields[1 + n]
        for m in range(n):
            extra = extra + tw[m] * fields[SUBITERS + n - m]
        numer_add[every, :] = extra

        @pl.loop(0, SWEEPS // 2)
        def _(p):
            step = n % 2 * SWEEPS + 2 * p
            sweep(state_a, state_b, step)
            sweep(state_b, state_a, step + 1)

        now = temp_a[every, :]
        tw[n] = now
        ext_c[...] = now[s_lo:s_hi, :].T
        for odd in range(2):
            pieces = split(ext_c[pl.ds(lo + odd, half, stride=2), :], PIECES)
            for p, piece in enumerate(pieces):
                at = (n * PIECES + p) * half
                wall[at : at + half, odd * cells_s : (odd + 1) * cells_s] = piece
        if n == 1:
            middle = across_span(
                temp_a, 8, PAD, SPAN_HALO, 16, (landing.at[1], landing.at[0])
            ) + across_span(
                tw.at[0], 1, 0, EDGE, 22, (landing_tw.at[1], landing_tw.at[0])
            )
            for copy in middle:
                copy.start()
            find(0)
            for copy in middle:
                copy.wait()
            for side, start in enumerate((s_lo - SPAN_HALO, s_hi)):
                at = (start + PAD) * 8
                temp_a[at : at + SPAN_HALO * 8, :] = landing[side]
                sides(start, state_a, SPAN_HALO)
                tw[0, side * s_hi : side * s_hi + EDGE, :] = landing_tw[side]
            tw[1] = temp_a[every, :]
    find(2)

    got = recv_fwd[...].reshape(LANES, LANES).T
    h = got[0:cap]
    tf = got[cap : 2 * cap]
    inv = 1.0 / (h + 2.0)
    for n in range(SUBITERS):
        q = h * (tf - 2.0 * slot_v[n])
        tf = tf - q * inv
    back = jnp.concatenate([q, tf, jnp.zeros((LANES - 2 * cap, LANES), f32)], axis=0)
    send_back[...] = back.T.reshape(LANES, 1, LANES)
    exchange(send_back, recv_back, 1)

    for l in range(layers):
        final = temp_a[pl.ds((PAD + s_lo) * 8 + l, cells_s, stride=8), :]
        solid_out[l] = 2.0 * final.T[lo:hi, :]

    arrived(send_back, recv_back, 1)
    table = recv_back[...].reshape(LANES, LANES).T[0 : 2 * cap]
    pieces = jnp.concatenate(split(table, 3), axis=0)
    for b in range(blocks):
        seen = nn(pieces, owner[:, b * LANES : (b + 1) * LANES])
        seen = seen[0 : 2 * cap] + seen[2 * cap : 4 * cap] + seen[4 * cap : 6 * cap]
        at_slot = slot_iota == rank[b : b + 1, :]
        q_row = jnp.sum(jnp.where(at_slot, seen[0:cap], 0.0), axis=0, keepdims=True)
        t_row = jnp.sum(jnp.where(at_slot, seen[cap : 2 * cap], 0.0), axis=0, keepdims=True)
        on = live[b : b + 1, :]
        flux_out[b : b + 1, :] = jnp.where(on, q_row, 0.0)
        fluid_out[b : b + 1, :] = jnp.where(on, t_row, fluid[b : b + 1, :])


def shards(
    n_blade,
    n_span,
    solid_temp,
    base_conductivity,
    coolant_htc,
    fluid_temp,
    wall_htc,
    face_dest,
    face_cell,
    face_count,
):
    layers, cells_x, cells_s = solid_temp.shape
    slots = fluid_temp.shape[0]
    cap = 32
    blocks = slots // LANES
    rows = cells_s + 2 * EDGE
    tall = rows + 2 * PAD
    vmem = pl.BlockSpec(memory_space=pltpu.VMEM)
    hbm = pl.BlockSpec(memory_space=pltpu.HBM)
    big = pltpu.VMEM((tall * 8, LANES), f32)
    faces_f = pltpu.VMEM((blocks, LANES), f32)
    faces_i = pltpu.VMEM((blocks, LANES), jnp.int32)
    faces = pltpu.VMEM((LANES, 1, LANES), f32)
    ext = pltpu.VMEM((layers, LANES, cells_s), f32)
    temp, fluid, flux = pl.pallas_call(
        functools.partial(kernel, n_blade, n_span, cap),
        out_shape=(
            jax.ShapeDtypeStruct(solid_temp.shape, f32),
            jax.ShapeDtypeStruct((blocks, LANES), f32),
            jax.ShapeDtypeStruct((blocks, LANES), f32),
        ),
        in_specs=[hbm] * 7 + [vmem],
        out_specs=(vmem, vmem, vmem),
        scratch_shapes=[
            faces_f,
            faces_f,
            faces_i,
            faces_i,
            ext,
            ext,
            pltpu.VMEM((LANES, cells_s), f32),
            ext,
            pltpu.VMEM((FIELDS * cells_x, 2 * cells_s), f32),
            [big] * 3,
            [big] * 3,
            big,
            big,
            big,
            pltpu.VMEM((rows, LANES), f32),
            pltpu.VMEM((FIELDS, rows, LANES), f32),
            big,
            big,
            pltpu.VMEM((SUBITERS, rows, LANES), f32),
            pltpu.VMEM((LANES, slots), bf16),
            pltpu.VMEM((blocks, LANES), f32),
            faces,
            faces,
            faces,
            faces,
            pltpu.VMEM((cap, LANES), jnp.int32),
            pltpu.VMEM((cap, LANES), jnp.int32),
            pltpu.VMEM((FIELDS, cap, LANES), f32),
            pltpu.VMEM((2 * cells_s, cap * LANES), bf16),
            pltpu.VMEM((SUBITERS * PIECES * cells_x // 2, 2 * cells_s), bf16),
            pltpu.SemaphoreType.DMA((7,)),
            pltpu.SemaphoreType.DMA((24,)),
            pltpu.SemaphoreType.DMA((24,)),
            pltpu.SemaphoreType.DMA((2,)),
            pltpu.SemaphoreType.DMA((2,)),
            pltpu.VMEM((2, SPAN_HALO * 8, LANES), f32),
            pltpu.VMEM((2, EDGE, LANES), f32),
        ],
        compiler_params=pltpu.CompilerParams(
            collective_id=0, has_side_effects=True, vmem_limit_bytes=67043328
        ),
    )(
        solid_temp,
        base_conductivity,
        coolant_htc,
        fluid_temp.reshape(blocks, LANES),
        wall_htc.reshape(blocks, LANES),
        face_dest.reshape(blocks, LANES),
        face_cell.reshape(blocks, LANES),
        face_count.reshape(1, 1),
    )
    return temp, fluid.reshape(slots), flux.reshape(slots)


def solution(mesh):
    placed = (
        P(None, "blade", "span"),
        P(None, "blade", "span"),
        P("blade", "span"),
        P(("blade", "span")),
        P(("blade", "span")),
        P(("blade", "span"), None),
        P(("blade", "span")),
        P(("blade", "span")),
    )
    return jax.shard_map(
        functools.partial(shards, mesh.shape["blade"], mesh.shape["span"]),
        mesh=mesh,
        in_specs=placed,
        out_specs=(P(None, "blade", "span"), P(("blade", "span")), P(("blade", "span"))),
        check_vma=False,
    )
```

```python
import functools

import jax
import jax.numpy as jnp
from jax import lax
from jax.experimental import pallas as pl
from jax.experimental.pallas import tpu as pltpu
from jax.sharding import PartitionSpec as P

SWEEPS = 6
SUBITERS = 4
HALO = SWEEPS * SUBITERS
LANES = 128
FIELDS = 2 * SUBITERS
PIECES = 3
CHUNK = 24
PAD = 24
SPAN_HALO = HALO // 2
EDGE = 16
MESH = pl.DeviceIdType.MESH
f32 = jnp.float32
bf16 = jnp.bfloat16


def iota(shape, dim):
    return lax.broadcasted_iota(jnp.int32, shape, dim)


def split(value, parts):
    pieces = []
    for _ in range(parts):
        piece = value.astype(bf16)
        pieces.append(piece)
        value = value - piece.astype(f32)
    return pieces


def nt(a, b):
    return lax.dot_general(a, b, (((1,), (1,)), ((), ())), preferred_element_type=f32)


def nn(a, b):
    return jnp.dot(a, b, preferred_element_type=f32)


def kernel(
    n_blade,
    n_span,
    cap,
    solid_ref,
    kappa_ref,
    cool_ref,
    fluid_ref,
    htc_ref,
    dest_ref,
    cell_ref,
    count_ref,
    solid_out,
    fluid_out,
    flux_out,
    fluid,
    htc,
    dest,
    cells,
    ext_t,
    ext_k,
    ext_c,
    ext_f,
    acc,
    state_a,
    state_b,
    rho,
    rho_up,
    rho_down,
    cool,
    fields,
    numer_add,
    denom_add,
    tw,
    owner,
    rank,
    send_fwd,
    recv_fwd,
    send_back,
    recv_back,
    slot_x,
    slot_s,
    slot_v,
    pick,
    wall,
    local_sem,
    halo_send,
    halo_recv,
    face_send,
    face_recv,
    landing,
    landing_tw,
):
    devices = n_blade * n_span
    layers, cells_x, cells_s = solid_ref.shape
    blocks = fluid_ref.shape[0]
    temp_a = state_a[0]
    ib, js = lax.axis_index("blade"), lax.axis_index("span")
    me = ib * n_span + js
    lo, hi = HALO, HALO + cells_x
    s_lo, s_hi = EDGE, EDGE + cells_s
    rows = cells_s + 2 * EDGE

    barrier = pltpu.get_barrier_semaphore()

    loads = [
        pltpu.make_async_copy(src, dst, local_sem.at[i])
        for i, (src, dst) in enumerate(
            (
                (dest_ref, dest),
                (cell_ref, cells),
                (htc_ref, htc),
                (fluid_ref, fluid),
                (solid_ref, ext_t.at[:, lo:hi, :]),
                (kappa_ref, ext_k.at[:, lo:hi, :]),
                (cool_ref, ext_c.at[lo:hi, :]),
            )
        )
    ]
    for load in loads:
        load.start()

    def peers(visit):
        unit = 7 if (devices - 1) % 7 == 1 else 1
        if unit > 1:
            visit_one(visit, devices - 1)

        @pl.loop(0, (devices - 1) // unit)
        def _(i):
            for j in range(unit):
                visit_one(visit, i * unit + j + 1)

    def visit_one(visit, k):
        peer = lax.rem(me + k, devices)
        visit(peer, (lax.div(peer, n_span), lax.rem(peer, n_span)))

    peers(
        lambda _, at: pl.semaphore_signal(barrier, inc=1, device_id=at, device_id_type=MESH)
    )
    for load in loads[:4]:
        load.wait()

    number = iota((blocks, LANES), 0) * LANES + iota((blocks, LANES), 1)
    live = number < jnp.broadcast_to(count_ref[...], (blocks, LANES))
    owner_row = jnp.where(live, dest[...], -1)
    before = (iota((LANES, 2 * LANES), 0) < iota((LANES, 2 * LANES), 1)) | (
        iota((LANES, 2 * LANES), 1) >= LANES
    )
    before = before.astype(f32).astype(bf16)
    dev_iota = iota((LANES, LANES), 0)
    offset = jnp.zeros((LANES, LANES), f32)
    packed = jnp.zeros((LANES, LANES), f32)
    cell_f = cells[...].astype(f32)
    slot_iota = iota((cap, LANES), 0).astype(f32)
    for b in range(blocks):
        mine = jnp.where(dev_iota == owner_row[b : b + 1, :], 1.0, 0.0)
        mine_b = mine.astype(bf16)
        owner[:, b * LANES : (b + 1) * LANES] = mine_b
        counts = nn(mine_b, before)
        order = jnp.sum(mine * (counts[:, :LANES] + offset), axis=0, keepdims=True)
        offset = offset + counts[:, LANES:]
        rank[b : b + 1, :] = order
        at_slot = slot_iota == order
        spread = jnp.concatenate(
            [
                jnp.where(at_slot, row[b : b + 1, :], 0.0)
                for row in (htc[...], fluid[...], cell_f)
            ]
            + [jnp.zeros((LANES - 3 * cap, LANES), f32)],
            axis=0,
        )
        for piece in split(spread, 3):
            packed = packed + nt(mine_b, piece)
    send_fwd[...] = packed.reshape(LANES, 1, LANES)
    if devices < LANES:
        recv_fwd[...] = jnp.zeros_like(recv_fwd)
        recv_back[...] = jnp.zeros_like(recv_back)

    pl.semaphore_wait(barrier, devices - 1)

    west = (lax.rem(ib + n_blade - 1, n_blade), js)
    east = (lax.rem(ib + 1, n_blade), js)
    south = (ib, lax.rem(js + n_span - 1, n_span))
    north = (ib, lax.rem(js + 1, n_span))

    def remote(src, dst, sem, to):
        return pltpu.make_async_remote_copy(
            src_ref=src,
            dst_ref=dst,
            send_sem=halo_send.at[sem],
            recv_sem=halo_recv.at[sem],
            device_id=to,
            device_id_type=MESH,
        )

    def across_blade(src, first, last, ext, sem):
        return (
            remote(src.at[..., first : first + HALO, :], ext.at[..., hi : hi + HALO, :], sem, west),
            remote(src.at[..., last - HALO : last, :], ext.at[..., 0:HALO, :], sem + 1, east),
        )

    x_halos = (
        across_blade(solid_ref, 0, cells_x, ext_t, 0)
        + across_blade(kappa_ref, 0, cells_x, ext_k, 2)
        + across_blade(cool_ref, 0, cells_x, ext_c, 4)
    )
    for copy in x_halos:
        copy.start()

    def exchange(send, recv, which):
        peers(
            lambda peer, at: pltpu.make_async_remote_copy(
                src_ref=send.at[peer],
                dst_ref=recv.at[me],
                send_sem=face_send.at[which],
                recv_sem=face_recv.at[which],
                device_id=at,
                device_id_type=MESH,
            ).start()
        )

        recv[pl.ds(me, 1)] = send[pl.ds(me, 1)]

    def arrived(send, recv, which):
        whole = pltpu.make_async_remote_copy(
            src_ref=send.at[pl.ds(0, devices - 1)],
            dst_ref=recv.at[pl.ds(0, devices - 1)],
            send_sem=face_send.at[which],
            recv_sem=face_recv.at[which],
            device_id=east,
            device_id_type=MESH,
        )
        whole.wait_send()
        whole.wait_recv()

    exchange(send_fwd, recv_fwd, 0)

    numer_add[...] = jnp.zeros_like(numer_add)
    denom_add[...] = jnp.zeros_like(denom_add)
    for load in loads[4:]:
        load.wait()
    for copy in x_halos:
        copy.wait()
    for l in range(layers):
        column = pl.ds((PAD + s_lo) * 8 + l, cells_s, stride=8)
        temp_a[column, :] = 0.5 * ext_t[l].T
        rho[column, :] = 1.0 / ext_k[l].T
    cool[s_lo:s_hi, :] = ext_c[...].T

    def across_span(ref, unit, pad, count, sem, land=None):
        first, last = (pad + s_lo) * unit, (pad + s_hi) * unit
        width = count * unit

        def part(start):
            if len(ref.shape) == 3:
                return ref.at[:, start : start + width, :]
            return ref.at[start : start + width, :]

        above, below = (part(last), part(first - width)) if land is None else land
        return (
            remote(part(first), above, sem, south),
            remote(part(last - width), below, sem + 1, north),
        )

    s_halos = (
        across_span(temp_a, 8, PAD, SPAN_HALO, 6)
        + across_span(rho, 8, PAD, SPAN_HALO, 8)
        + across_span(cool, 1, 0, EDGE, 10)
    )
    for copy in s_halos:
        copy.start()

    arrived(send_fwd, recv_fwd, 0)
    got = recv_fwd[...].reshape(LANES, LANES).T
    h = got[0:cap]
    tf = got[cap : 2 * cap]
    cell = got[2 * cap : 3 * cap].astype(jnp.int32)
    x_cell = cell // cells_s
    slot_x[...] = x_cell // 2
    slot_s[...] = cell - (x_cell // 2) * (2 * cells_s)
    inv = 1.0 / (h + 2.0)
    keep = 2.0 * inv
    value = 0.5 * h
    slot_v[0] = value
    value = 0.25 * h * tf
    for n in range(SUBITERS):
        slot_v[1 + n] = value
        value = value * keep
    value = 0.5 * h * (h * inv)
    for n in range(SUBITERS - 1):
        slot_v[1 + SUBITERS + n] = value
        value = value * keep
    acc[...] = jnp.zeros_like(acc)
    half = cells_x // 2
    x_iota = iota((half, LANES), 0)
    s_iota = iota((2 * cells_s, LANES), 0)
    group = 4

    def scatter(fresh, chosen):
        span = 2 * len(chosen) * half
        base = 2 * chosen[0] * half

        @pl.loop(0, cap // group)
        def _(g):
            lhs, rhs = [], []
            for j in range(group):
                r = g * group + j
                row = pl.ds(r, 1)
                lanes = pl.ds(pl.multiple_of(r * LANES, LANES), LANES)
                if fresh:
                    s_hit = jnp.where(s_iota == slot_s[row, :], 1.0, 0.0).astype(bf16)
                    pick[:, lanes] = s_hit
                else:
                    s_hit = pick[:, lanes]
                x_hit = x_iota == slot_x[row, :]
                upper, lower = [], []
                for k in chosen:
                    v = slot_v[k, row, :]
                    v_up = v.astype(bf16).astype(f32)
                    upper.append(jnp.where(x_hit, v_up, 0.0).astype(bf16))
                    lower.append(jnp.where(x_hit, v - v_up, 0.0).astype(bf16))
                lhs.append(jnp.concatenate(upper + lower, axis=0))
                rhs.append(s_hit)
            acc[base : base + span, :] += nt(
                jnp.concatenate(lhs, axis=1), jnp.concatenate(rhs, axis=1)
            )

        for i, k in enumerate(chosen):
            for odd in range(2):
                lanes = slice(odd * cells_s, (odd + 1) * cells_s)
                up = base + i * half
                low = up + len(chosen) * half
                ext_f[k, pl.ds(lo + odd, half, stride=2), :] = (
                    acc[up : up + half, lanes] + acc[low : low + half, lanes]
                )

    def turn(chosen):
        for k in chosen:
            fields[k, s_lo:s_hi, :] = ext_f[k].T

    soon, later = range(0, 2), range(2, FIELDS)
    ext_soon, ext_later = ext_f.at[0:2], ext_f.at[2:FIELDS]
    scatter(True, soon)
    f_x = across_blade(ext_soon, lo, hi, ext_soon, 12)
    for copy in f_x:
        copy.start()
    scatter(False, later)
    late_x = across_blade(ext_later, lo, hi, ext_later, 18)
    for copy in late_x:
        copy.start()

    lane = iota((8, LANES), 1)
    inside_x = ((lane >= lo) | (ib > 0)) & ((lane < hi) | (ib < n_blade - 1))

    def tile(s):
        return pl.ds(pl.multiple_of((s + PAD) * 8, 8), 8)

    def sides(s, to, count=CHUNK):
        for j in range(count):
            at = tile(s + j)
            t = to[0][at, :]
            to[1][at, :] = pltpu.roll(t, LANES - 1, 1)
            to[2][at, :] = pltpu.roll(t, 1, 1)

    def fill(i):
        inside = inside_x & (
            ((i >= s_lo // 8) | (js > 0)) & ((i < s_hi // 8) | (js < n_span - 1))
        )
        for j in range(8):
            at = tile(i * 8 + j)
            held = jnp.where(inside, rho[at, :], 1e15)
            rho[at, :] = held
            rho_up[at, :] = pltpu.roll(held, LANES - 1, 1)
            rho_down[at, :] = pltpu.roll(held, 1, 1)
        sides(i * 8, state_a, 8)

    edge = EDGE // 8

    @pl.loop(2 * edge, rows // 8 - 2 * edge)
    def _(i):
        fill(i)

    for copy in f_x:
        copy.wait()
    turn(soon)
    f_s = across_span(fields.at[0:2], 1, 0, EDGE, 14)
    for copy in f_s:
        copy.start()
    for copy in s_halos:
        copy.wait()

    @pl.loop(0, 2 * edge)
    def _(i):
        fill(i)
        fill(i + rows // 8 - 2 * edge)

    for copy in late_x:
        copy.wait()
    turn(later)
    late_s = across_span(fields.at[2:FIELDS], 1, 0, EDGE, 20)
    for copy in late_s:
        copy.start()
    for copy in f_s:
        copy.wait()

    every = pl.ds(PAD * 8, rows, stride=8)
    denom_add[every, :] = fields[0]
    denom_add[pl.ds(PAD * 8 + layers - 1, rows, stride=8), :] = 0.5 * cool[...]
    not_last = jnp.where(iota((8, LANES), 0) < layers - 1, 1.0, 0.0)

    def sweep(src, dst, step):
        first = EDGE - SPAN_HALO + 1 + step

        def chunk(i, carry):
            t_prev, t_here, r_here, w_prev = carry
            start = first + i * CHUNK
            sides(start - CHUNK, dst)
            for j in range(CHUNK):
                at, after = tile(start + j), tile(start + j + 1)
                t_next = src[0][after, :]
                r_next = resist(t_next, rho[after, :])
                t_up, t_down = src[1][at, :], src[2][at, :]
                w_next = 1.0 / (r_here + r_next)
                w_up = 1.0 / (r_here + resist(t_up, rho_up[at, :]))
                w_down = 1.0 / (r_here + resist(t_down, rho_down[at, :]))
                w_in = not_last / (r_here + pltpu.roll(r_here, 7, 0))
                w_out = pltpu.roll(w_in, 1, 0)
                numer = (
                    (w_next * t_next + w_prev * t_prev)
                    + (w_up * t_up + w_down * t_down)
                    + (w_in * pltpu.roll(t_here, 7, 0) + w_out * pltpu.roll(t_here, 1, 0))
                    + numer_add[at, :]
                )
                denom = ((w_next + w_prev) + (w_up + w_down)) + (
                    (w_in + w_out) + denom_add[at, :]
                )
                dst[0][at, :] = numer / denom
                t_prev, t_here, r_here, w_prev = t_here, t_next, r_next, w_next
            return t_prev, t_here, r_here, w_prev

        def resist(t, held):
            return held / (1.0 + t * t)

        before, here = tile(first - 1), tile(first)
        t_prev, t_here = src[0][before, :], src[0][here, :]
        r_here = resist(t_here, rho[here, :])
        w_prev = 1.0 / (resist(t_prev, rho[before, :]) + r_here)
        count = (rows - 2 * first + CHUNK - 1) // CHUNK
        lax.fori_loop(0, count, chunk, (t_prev, t_here, r_here, w_prev))
        sides(first + (count - 1) * CHUNK, dst)

    def find(early):
        pair = 2 * PIECES * half

        @pl.loop(0, cap // group)
        def _(g):
            width = group * LANES
            lanes = pl.ds(pl.multiple_of(g * width, width), width)
            found = nn(wall[early * PIECES * half : early * PIECES * half + pair, :], pick[:, lanes])
            for j in range(group):
                row = pl.ds(g * group + j, 1)
                x_hit = x_iota == slot_x[row, :]
                for n in range(2):
                    at = n * PIECES * half
                    total = found[at : at + half, j * LANES : (j + 1) * LANES]
                    for p in range(1, PIECES):
                        total = total + found[
                            at + p * half : at + (p + 1) * half, j * LANES : (j + 1) * LANES
                        ]
                    slot_v[early + n, row, :] = jnp.sum(
                        jnp.where(x_hit, total, 0.0), axis=0, keepdims=True
                    )

    for n in range(SUBITERS):
        if n == 1:
            for copy in late_s:
                copy.wait()
        extra = fields[1 + n]
        for m in range(n):
            extra = extra + tw[m] * fields[SUBITERS + n - m]
        numer_add[every, :] = extra

        @pl.loop(0, SWEEPS // 2)
        def _(p):
            step = n % 2 * SWEEPS + 2 * p
            sweep(state_a, state_b, step)
            sweep(state_b, state_a, step + 1)

        now = temp_a[every, :]
        tw[n] = now
        ext_c[...] = now[s_lo:s_hi, :].T
        for odd in range(2):
            pieces = split(ext_c[pl.ds(lo + odd, half, stride=2), :], PIECES)
            for p, piece in enumerate(pieces):
                at = (n * PIECES + p) * half
                wall[at : at + half, odd * cells_s : (odd + 1) * cells_s] = piece
        if n == 1:
            middle = across_span(
                temp_a, 8, PAD, SPAN_HALO, 16, (landing.at[1], landing.at[0])
            ) + across_span(
                tw.at[0], 1, 0, EDGE, 22, (landing_tw.at[1], landing_tw.at[0])
            )
            for copy in middle:
                copy.start()
            find(0)
            for copy in middle:
                copy.wait()
            for side, start in enumerate((s_lo - SPAN_HALO, s_hi)):
                at = (start + PAD) * 8
                temp_a[at : at + SPAN_HALO * 8, :] = landing[side]
                sides(start, state_a, SPAN_HALO)
                tw[0, side * s_hi : side * s_hi + EDGE, :] = landing_tw[side]
            tw[1] = temp_a[every, :]
    find(2)

    got = recv_fwd[...].reshape(LANES, LANES).T
    h = got[0:cap]
    tf = got[cap : 2 * cap]
    inv = 1.0 / (h + 2.0)
    for n in range(SUBITERS):
        q = h * (tf - 2.0 * slot_v[n])
        tf = tf - q * inv
    back = jnp.concatenate([q, tf, jnp.zeros((LANES - 2 * cap, LANES), f32)], axis=0)
    send_back[...] = back.T.reshape(LANES, 1, LANES)
    exchange(send_back, recv_back, 1)

    for l in range(layers):
        final = temp_a[pl.ds((PAD + s_lo) * 8 + l, cells_s, stride=8), :]
        ext_k[l, 0:cells_x, :] = 2.0 * final.T[lo:hi, :]
    store = pltpu.make_async_copy(ext_k.at[:, 0:cells_x, :], solid_out, local_sem.at[0])
    store.start()

    arrived(send_back, recv_back, 1)
    table = recv_back[...].reshape(LANES, LANES).T[0 : 2 * cap]
    pieces = jnp.concatenate(split(table, 3), axis=0)
    for b in range(blocks):
        seen = nn(pieces, owner[:, b * LANES : (b + 1) * LANES])
        seen = seen[0 : 2 * cap] + seen[2 * cap : 4 * cap] + seen[4 * cap : 6 * cap]
        at_slot = slot_iota == rank[b : b + 1, :]
        q_row = jnp.sum(jnp.where(at_slot, seen[0:cap], 0.0), axis=0, keepdims=True)
        t_row = jnp.sum(jnp.where(at_slot, seen[cap : 2 * cap], 0.0), axis=0, keepdims=True)
        on = live[b : b + 1, :]
        flux_out[b : b + 1, :] = jnp.where(on, q_row, 0.0)
        fluid_out[b : b + 1, :] = jnp.where(on, t_row, fluid[b : b + 1, :])
    store.wait()


def shards(
    n_blade,
    n_span,
    solid_temp,
    base_conductivity,
    coolant_htc,
    fluid_temp,
    wall_htc,
    face_dest,
    face_cell,
    face_count,
):
    layers, cells_x, cells_s = solid_temp.shape
    slots = fluid_temp.shape[0]
    cap = 32
    blocks = slots // LANES
    rows = cells_s + 2 * EDGE
    tall = rows + 2 * PAD
    vmem = pl.BlockSpec(memory_space=pltpu.VMEM)
    hbm = pl.BlockSpec(memory_space=pltpu.HBM)
    big = pltpu.VMEM((tall * 8, LANES), f32)
    faces_f = pltpu.VMEM((blocks, LANES), f32)
    faces_i = pltpu.VMEM((blocks, LANES), jnp.int32)
    faces = pltpu.VMEM((LANES, 1, LANES), f32)
    ext = pltpu.VMEM((layers, LANES, cells_s), f32)
    temp, fluid, flux = pl.pallas_call(
        functools.partial(kernel, n_blade, n_span, cap),
        out_shape=(
            jax.ShapeDtypeStruct(solid_temp.shape, f32),
            jax.ShapeDtypeStruct((blocks, LANES), f32),
            jax.ShapeDtypeStruct((blocks, LANES), f32),
        ),
        in_specs=[hbm] * 7 + [vmem],
        out_specs=(hbm, vmem, vmem),
        scratch_shapes=[
            faces_f,
            faces_f,
            faces_i,
            faces_i,
            ext,
            ext,
            pltpu.VMEM((LANES, cells_s), f32),
            ext,
            pltpu.VMEM((FIELDS * cells_x, 2 * cells_s), f32),
            [big] * 3,
            [big] * 3,
            big,
            big,
            big,
            pltpu.VMEM((rows, LANES), f32),
            pltpu.VMEM((FIELDS, rows, LANES), f32),
            big,
            big,
            pltpu.VMEM((SUBITERS, rows, LANES), f32),
            pltpu.VMEM((LANES, slots), bf16),
            pltpu.VMEM((blocks, LANES), f32),
            faces,
            faces,
            faces,
            faces,
            pltpu.VMEM((cap, LANES), jnp.int32),
            pltpu.VMEM((cap, LANES), jnp.int32),
            pltpu.VMEM((FIELDS, cap, LANES), f32),
            pltpu.VMEM((2 * cells_s, cap * LANES), bf16),
            pltpu.VMEM((SUBITERS * PIECES * cells_x // 2, 2 * cells_s), bf16),
            pltpu.SemaphoreType.DMA((7,)),
            pltpu.SemaphoreType.DMA((24,)),
            pltpu.SemaphoreType.DMA((24,)),
            pltpu.SemaphoreType.DMA((2,)),
            pltpu.SemaphoreType.DMA((2,)),
            pltpu.VMEM((2, SPAN_HALO * 8, LANES), f32),
            pltpu.VMEM((2, EDGE, LANES), f32),
        ],
        compiler_params=pltpu.CompilerParams(
            collective_id=0, has_side_effects=True, vmem_limit_bytes=67043328
        ),
    )(
        solid_temp,
        base_conductivity,
        coolant_htc,
        fluid_temp.reshape(blocks, LANES),
        wall_htc.reshape(blocks, LANES),
        face_dest.reshape(blocks, LANES),
        face_cell.reshape(blocks, LANES),
        face_count.reshape(1, 1),
    )
    return temp, fluid.reshape(slots), flux.reshape(slots)


def solution(mesh):
    placed = (
        P(None, "blade", "span"),
        P(None, "blade", "span"),
        P("blade", "span"),
        P(("blade", "span")),
        P(("blade", "span")),
        P(("blade", "span"), None),
        P(("blade", "span")),
        P(("blade", "span")),
    )
    return jax.shard_map(
        functools.partial(shards, mesh.shape["blade"], mesh.shape["span"]),
        mesh=mesh,
        in_specs=placed,
        out_specs=(P(None, "blade", "span"), P(("blade", "span")), P(("blade", "span"))),
        check_vma=False,
    )
```

```python
import functools

import jax
import jax.numpy as jnp
from jax import lax
from jax.experimental import pallas as pl
from jax.experimental.pallas import tpu as pltpu
from jax.sharding import PartitionSpec as P

SWEEPS = 6
SUBITERS = 4
HALO = SWEEPS * SUBITERS
LANES = 128
FIELDS = 2 * SUBITERS
PIECES = 3
CHUNK = 24
PAD = 24
SPAN_HALO = HALO // 2
EDGE = 16
MESH = pl.DeviceIdType.MESH
f32 = jnp.float32
bf16 = jnp.bfloat16


def iota(shape, dim):
    return lax.broadcasted_iota(jnp.int32, shape, dim)


def split(value, parts):
    pieces = []
    for _ in range(parts):
        piece = value.astype(bf16)
        pieces.append(piece)
        value = value - piece.astype(f32)
    return pieces


def nt(a, b):
    return lax.dot_general(a, b, (((1,), (1,)), ((), ())), preferred_element_type=f32)


def nn(a, b):
    return jnp.dot(a, b, preferred_element_type=f32)


def kernel(
    n_blade,
    n_span,
    cap,
    solid_ref,
    kappa_ref,
    cool_ref,
    fluid_ref,
    htc_ref,
    dest_ref,
    cell_ref,
    count_ref,
    solid_out,
    fluid_out,
    flux_out,
    fluid,
    htc,
    dest,
    cells,
    ext_t,
    ext_k,
    ext_c,
    ext_f,
    acc,
    state_a,
    state_b,
    rho,
    rho_up,
    rho_down,
    cool,
    fields,
    numer_add,
    denom_add,
    tw,
    owner,
    rank,
    send_fwd,
    recv_fwd,
    send_back,
    recv_back,
    slot_x,
    slot_s,
    slot_v,
    pick,
    wall,
    local_sem,
    halo_send,
    halo_recv,
    face_send,
    face_recv,
    landing,
    landing_tw,
):
    devices = n_blade * n_span
    layers, cells_x, cells_s = solid_ref.shape
    blocks = fluid_ref.shape[0]
    temp_a = state_a[0]
    ib, js = lax.axis_index("blade"), lax.axis_index("span")
    me = ib * n_span + js
    lo, hi = HALO, HALO + cells_x
    s_lo, s_hi = EDGE, EDGE + cells_s
    rows = cells_s + 2 * EDGE

    barrier = pltpu.get_barrier_semaphore()

    loads = [
        pltpu.make_async_copy(src, dst, local_sem.at[i])
        for i, (src, dst) in enumerate(
            (
                (dest_ref, dest),
                (cell_ref, cells),
                (htc_ref, htc),
                (fluid_ref, fluid),
                (solid_ref, ext_t.at[:, lo:hi, :]),
                (kappa_ref, ext_k.at[:, lo:hi, :]),
                (cool_ref, ext_c.at[lo:hi, :]),
            )
        )
    ]
    for load in loads:
        load.start()

    def peers(visit):
        unit = 7 if (devices - 1) % 7 == 1 else 1
        if unit > 1:
            visit_one(visit, devices - 1)

        @pl.loop(0, (devices - 1) // unit)
        def _(i):
            for j in range(unit):
                visit_one(visit, i * unit + j + 1)

    def visit_one(visit, k):
        peer = lax.rem(me + k, devices)
        visit(peer, (lax.div(peer, n_span), lax.rem(peer, n_span)))

    peers(
        lambda _, at: pl.semaphore_signal(barrier, inc=1, device_id=at, device_id_type=MESH)
    )
    for load in loads[:4]:
        load.wait()

    number = iota((blocks, LANES), 0) * LANES + iota((blocks, LANES), 1)
    live = number < jnp.broadcast_to(count_ref[...], (blocks, LANES))
    owner_row = jnp.where(live, dest[...], -1)
    before = (iota((LANES, 2 * LANES), 0) < iota((LANES, 2 * LANES), 1)) | (
        iota((LANES, 2 * LANES), 1) >= LANES
    )
    before = before.astype(f32).astype(bf16)
    dev_iota = iota((LANES, LANES), 0)
    offset = jnp.zeros((LANES, LANES), f32)
    packed = jnp.zeros((LANES, LANES), f32)
    cell_f = cells[...].astype(f32)
    slot_iota = iota((cap, LANES), 0).astype(f32)
    for b in range(blocks):
        mine = jnp.where(dev_iota == owner_row[b : b + 1, :], 1.0, 0.0)
        mine_b = mine.astype(bf16)
        owner[:, b * LANES : (b + 1) * LANES] = mine_b
        counts = nn(mine_b, before)
        order = jnp.sum(mine * (counts[:, :LANES] + offset), axis=0, keepdims=True)
        offset = offset + counts[:, LANES:]
        rank[b : b + 1, :] = order
        at_slot = slot_iota == order
        spread = jnp.concatenate(
            [
                jnp.where(at_slot, row[b : b + 1, :], 0.0)
                for row in (htc[...], fluid[...], cell_f)
            ]
            + [jnp.zeros((LANES - 3 * cap, LANES), f32)],
            axis=0,
        )
        for piece in split(spread, 3):
            packed = packed + nt(mine_b, piece)
    send_fwd[...] = packed.reshape(LANES, 1, LANES)
    if devices < LANES:
        recv_fwd[...] = jnp.zeros_like(recv_fwd)
        recv_back[...] = jnp.zeros_like(recv_back)

    pl.semaphore_wait(barrier, devices - 1)

    west = (lax.rem(ib + n_blade - 1, n_blade), js)
    east = (lax.rem(ib + 1, n_blade), js)
    south = (ib, lax.rem(js + n_span - 1, n_span))
    north = (ib, lax.rem(js + 1, n_span))

    def remote(src, dst, sem, to):
        return pltpu.make_async_remote_copy(
            src_ref=src,
            dst_ref=dst,
            send_sem=halo_send.at[sem],
            recv_sem=halo_recv.at[sem],
            device_id=to,
            device_id_type=MESH,
        )

    def across_blade(src, first, last, ext, sem):
        return (
            remote(src.at[..., first : first + HALO, :], ext.at[..., hi : hi + HALO, :], sem, west),
            remote(src.at[..., last - HALO : last, :], ext.at[..., 0:HALO, :], sem + 1, east),
        )

    x_halos = (
        across_blade(solid_ref, 0, cells_x, ext_t, 0)
        + across_blade(kappa_ref, 0, cells_x, ext_k, 2)
        + across_blade(cool_ref, 0, cells_x, ext_c, 4)
    )
    for copy in x_halos:
        copy.start()

    def exchange(send, recv, which):
        peers(
            lambda peer, at: pltpu.make_async_remote_copy(
                src_ref=send.at[peer],
                dst_ref=recv.at[me],
                send_sem=face_send.at[which],
                recv_sem=face_recv.at[which],
                device_id=at,
                device_id_type=MESH,
            ).start()
        )

        recv[pl.ds(me, 1)] = send[pl.ds(me, 1)]

    def arrived(send, recv, which):
        whole = pltpu.make_async_remote_copy(
            src_ref=send.at[pl.ds(0, devices - 1)],
            dst_ref=recv.at[pl.ds(0, devices - 1)],
            send_sem=face_send.at[which],
            recv_sem=face_recv.at[which],
            device_id=east,
            device_id_type=MESH,
        )
        whole.wait_send()
        whole.wait_recv()

    exchange(send_fwd, recv_fwd, 0)

    numer_add[...] = jnp.zeros_like(numer_add)
    denom_add[...] = jnp.zeros_like(denom_add)
    for load in loads[4:]:
        load.wait()
    for copy in x_halos:
        copy.wait()
    for l in range(layers):
        column = pl.ds((PAD + s_lo) * 8 + l, cells_s, stride=8)
        temp_a[column, :] = 0.5 * ext_t[l].T
        rho[column, :] = 1.0 / ext_k[l].T
    cool[s_lo:s_hi, :] = ext_c[...].T

    def across_span(ref, unit, pad, count, sem, land=None):
        first, last = (pad + s_lo) * unit, (pad + s_hi) * unit
        width = count * unit

        def part(start):
            if len(ref.shape) == 3:
                return ref.at[:, start : start + width, :]
            return ref.at[start : start + width, :]

        above, below = (part(last), part(first - width)) if land is None else land
        return (
            remote(part(first), above, sem, south),
            remote(part(last - width), below, sem + 1, north),
        )

    s_halos = (
        across_span(temp_a, 8, PAD, SPAN_HALO, 6)
        + across_span(rho, 8, PAD, SPAN_HALO, 8)
        + across_span(cool, 1, 0, EDGE, 10)
    )
    for copy in s_halos:
        copy.start()

    arrived(send_fwd, recv_fwd, 0)
    got = recv_fwd[...].reshape(LANES, LANES).T
    h = got[0:cap]
    tf = got[cap : 2 * cap]
    cell = got[2 * cap : 3 * cap].astype(jnp.int32)
    x_cell = cell // cells_s
    slot_x[...] = x_cell // 2
    slot_s[...] = cell - (x_cell // 2) * (2 * cells_s)
    inv = 1.0 / (h + 2.0)
    keep = 2.0 * inv
    value = 0.5 * h
    slot_v[0] = value
    value = 0.25 * h * tf
    for n in range(SUBITERS):
        slot_v[1 + n] = value
        value = value * keep
    value = 0.5 * h * (h * inv)
    for n in range(SUBITERS - 1):
        slot_v[1 + SUBITERS + n] = value
        value = value * keep
    acc[...] = jnp.zeros_like(acc)
    half = cells_x // 2
    x_iota = iota((half, LANES), 0)
    s_iota = iota((2 * cells_s, LANES), 0)
    group = 4

    def scatter(fresh, chosen):
        span = 2 * len(chosen) * half
        base = 2 * chosen[0] * half

        @pl.loop(0, cap // group)
        def _(g):
            lhs, rhs = [], []
            for j in range(group):
                r = g * group + j
                row = pl.ds(r, 1)
                lanes = pl.ds(pl.multiple_of(r * LANES, LANES), LANES)
                if fresh:
                    s_hit = jnp.where(s_iota == slot_s[row, :], 1.0, 0.0).astype(bf16)
                    pick[:, lanes] = s_hit
                else:
                    s_hit = pick[:, lanes]
                x_hit = x_iota == slot_x[row, :]
                upper, lower = [], []
                for k in chosen:
                    v = slot_v[k, row, :]
                    v_up = v.astype(bf16).astype(f32)
                    upper.append(jnp.where(x_hit, v_up, 0.0).astype(bf16))
                    lower.append(jnp.where(x_hit, v - v_up, 0.0).astype(bf16))
                lhs.append(jnp.concatenate(upper + lower, axis=0))
                rhs.append(s_hit)
            acc[base : base + span, :] += nt(
                jnp.concatenate(lhs, axis=1), jnp.concatenate(rhs, axis=1)
            )

        for i, k in enumerate(chosen):
            for odd in range(2):
                lanes = slice(odd * cells_s, (odd + 1) * cells_s)
                up = base + i * half
                low = up + len(chosen) * half
                ext_f[k, pl.ds(lo + odd, half, stride=2), :] = (
                    acc[up : up + half, lanes] + acc[low : low + half, lanes]
                )

    def turn(chosen):
        for k in chosen:
            fields[k, s_lo:s_hi, :] = ext_f[k].T

    soon, later = range(0, 2), range(2, FIELDS)
    ext_soon, ext_later = ext_f.at[0:2], ext_f.at[2:FIELDS]
    scatter(True, soon)
    f_x = across_blade(ext_soon, lo, hi, ext_soon, 12)
    for copy in f_x:
        copy.start()
    scatter(False, later)
    late_x = across_blade(ext_later, lo, hi, ext_later, 18)
    for copy in late_x:
        copy.start()

    lane = iota((8, LANES), 1)
    inside_x = ((lane >= lo) | (ib > 0)) & ((lane < hi) | (ib < n_blade - 1))

    def tile(s):
        return pl.ds(pl.multiple_of((s + PAD) * 8, 8), 8)

    def sides(s, to, count=CHUNK):
        for j in range(count):
            at = tile(s + j)
            t = to[0][at, :]
            to[1][at, :] = pltpu.roll(t, LANES - 1, 1)
            to[2][at, :] = pltpu.roll(t, 1, 1)

    def fill(i):
        inside = inside_x & (
            ((i >= s_lo // 8) | (js > 0)) & ((i < s_hi // 8) | (js < n_span - 1))
        )
        for j in range(8):
            at = tile(i * 8 + j)
            held = jnp.where(inside, rho[at, :], 1e15)
            rho[at, :] = held
            rho_up[at, :] = pltpu.roll(held, LANES - 1, 1)
            rho_down[at, :] = pltpu.roll(held, 1, 1)
        sides(i * 8, state_a, 8)

    edge = EDGE // 8

    @pl.loop(2 * edge, rows // 8 - 2 * edge)
    def _(i):
        fill(i)

    for copy in f_x:
        copy.wait()
    turn(soon)
    f_s = across_span(fields.at[0:2], 1, 0, EDGE, 14)
    for copy in f_s:
        copy.start()
    for copy in s_halos:
        copy.wait()

    @pl.loop(0, 2 * edge)
    def _(i):
        fill(i)
        fill(i + rows // 8 - 2 * edge)

    for copy in late_x:
        copy.wait()
    turn(later)
    late_s = across_span(fields.at[2:FIELDS], 1, 0, EDGE, 20)
    for copy in late_s:
        copy.start()
    for copy in f_s:
        copy.wait()

    every = pl.ds(PAD * 8, rows, stride=8)
    denom_add[every, :] = fields[0]
    denom_add[pl.ds(PAD * 8 + layers - 1, rows, stride=8), :] = 0.5 * cool[...]
    not_last = jnp.where(iota((8, LANES), 0) < layers - 1, 1.0, 0.0)

    def chunks(first):
        return (rows - 2 * first + CHUNK - 1) // CHUNK

    def last_chunk(first):
        return first + (chunks(first) - 1) * CHUNK

    def sweep(src, dst, step):
        first = EDGE - SPAN_HALO + 1 + step

        def chunk(i, carry, done=None):
            t_prev, t_here, r_here, w_prev = carry
            start = first + i * CHUNK
            if done is None:
                sides(start - CHUNK, dst)
            for j in range(CHUNK):
                at, after = tile(start + j), tile(start + j + 1)
                t_next = src[0][after, :]
                r_next = resist(t_next, rho[after, :])
                t_up, t_down = src[1][at, :], src[2][at, :]
                w_next = 1.0 / (r_here + r_next)
                w_up = 1.0 / (r_here + resist(t_up, rho_up[at, :]))
                w_down = 1.0 / (r_here + resist(t_down, rho_down[at, :]))
                w_in = not_last / (r_here + pltpu.roll(r_here, 7, 0))
                w_out = pltpu.roll(w_in, 1, 0)
                numer = (
                    (w_next * t_next + w_prev * t_prev)
                    + (w_up * t_up + w_down * t_down)
                    + (w_in * pltpu.roll(t_here, 7, 0) + w_out * pltpu.roll(t_here, 1, 0))
                    + numer_add[at, :]
                )
                denom = ((w_next + w_prev) + (w_up + w_down)) + (
                    (w_in + w_out) + denom_add[at, :]
                )
                dst[0][at, :] = numer / denom
                t_prev, t_here, r_here, w_prev = t_here, t_next, r_next, w_next
            if done is not None:
                sides(done, src)
            return t_prev, t_here, r_here, w_prev

        def resist(t, held):
            return held / (1.0 + t * t)

        before, here = tile(first - 1), tile(first)
        t_prev, t_here = src[0][before, :], src[0][here, :]
        r_here = resist(t_here, rho[here, :])
        w_prev = 1.0 / (resist(t_prev, rho[before, :]) + r_here)
        carry = chunk(0, (t_prev, t_here, r_here, w_prev), last_chunk(first - 1))
        lax.fori_loop(1, chunks(first), chunk, carry)

    def find(early):
        pair = 2 * PIECES * half

        @pl.loop(0, cap // 8)
        def _(g):
            width = 8 * LANES
            lanes = pl.ds(pl.multiple_of(g * width, width), width)
            found = nn(wall[early * PIECES * half : early * PIECES * half + pair, :], pick[:, lanes])
            for j in range(8):
                row = pl.ds(g * 8 + j, 1)
                x_hit = x_iota == slot_x[row, :]
                for n in range(2):
                    at = n * PIECES * half
                    total = found[at : at + half, j * LANES : (j + 1) * LANES]
                    for p in range(1, PIECES):
                        total = total + found[
                            at + p * half : at + (p + 1) * half, j * LANES : (j + 1) * LANES
                        ]
                    slot_v[early + n, row, :] = jnp.sum(
                        jnp.where(x_hit, total, 0.0), axis=0, keepdims=True
                    )

    for n in range(SUBITERS):
        if n == 1:
            for copy in late_s:
                copy.wait()
        extra = fields[1 + n]
        for m in range(n):
            extra = extra + tw[m] * fields[SUBITERS + n - m]
        numer_add[every, :] = extra

        @pl.loop(0, SWEEPS // 2)
        def _(p):
            step = n % 2 * SWEEPS + 2 * p
            sweep(state_a, state_b, step)
            sweep(state_b, state_a, step + 1)

        now = temp_a[every, :]
        tw[n] = now
        ext_c[...] = now[s_lo:s_hi, :].T
        for odd in range(2):
            pieces = split(ext_c[pl.ds(lo + odd, half, stride=2), :], PIECES)
            for p, piece in enumerate(pieces):
                at = (n * PIECES + p) * half
                wall[at : at + half, odd * cells_s : (odd + 1) * cells_s] = piece
        if n == 1:
            middle = across_span(
                temp_a, 8, PAD, SPAN_HALO, 16, (landing.at[1], landing.at[0])
            ) + across_span(
                tw.at[0], 1, 0, EDGE, 22, (landing_tw.at[1], landing_tw.at[0])
            )
            for copy in middle:
                copy.start()
            find(0)
            sides(last_chunk(s_lo), state_a)
            for copy in middle:
                copy.wait()
            for side, start in enumerate((s_lo - SPAN_HALO, s_hi)):
                at = (start + PAD) * 8
                temp_a[at : at + SPAN_HALO * 8, :] = landing[side]
                sides(start, state_a, SPAN_HALO)
                tw[0, side * s_hi : side * s_hi + EDGE, :] = landing_tw[side]
            tw[1] = temp_a[every, :]
    find(2)

    got = recv_fwd[...].reshape(LANES, LANES).T
    h = got[0:cap]
    tf = got[cap : 2 * cap]
    inv = 1.0 / (h + 2.0)
    for n in range(SUBITERS):
        q = h * (tf - 2.0 * slot_v[n])
        tf = tf - q * inv
    back = jnp.concatenate([q, tf, jnp.zeros((LANES - 2 * cap, LANES), f32)], axis=0)
    send_back[...] = back.T.reshape(LANES, 1, LANES)
    exchange(send_back, recv_back, 1)

    for l in range(layers):
        final = temp_a[pl.ds((PAD + s_lo) * 8 + l, cells_s, stride=8), :]
        ext_k[l, 0:cells_x, :] = 2.0 * final.T[lo:hi, :]
    store = pltpu.make_async_copy(ext_k.at[:, 0:cells_x, :], solid_out, local_sem.at[0])
    store.start()

    arrived(send_back, recv_back, 1)
    table = recv_back[...].reshape(LANES, LANES).T[0 : 2 * cap]
    pieces = jnp.concatenate(split(table, 3), axis=0)
    for b in range(blocks):
        seen = nn(pieces, owner[:, b * LANES : (b + 1) * LANES])
        seen = seen[0 : 2 * cap] + seen[2 * cap : 4 * cap] + seen[4 * cap : 6 * cap]
        at_slot = slot_iota == rank[b : b + 1, :]
        q_row = jnp.sum(jnp.where(at_slot, seen[0:cap], 0.0), axis=0, keepdims=True)
        t_row = jnp.sum(jnp.where(at_slot, seen[cap : 2 * cap], 0.0), axis=0, keepdims=True)
        on = live[b : b + 1, :]
        flux_out[b : b + 1, :] = jnp.where(on, q_row, 0.0)
        fluid_out[b : b + 1, :] = jnp.where(on, t_row, fluid[b : b + 1, :])
    store.wait()


def shards(
    n_blade,
    n_span,
    solid_temp,
    base_conductivity,
    coolant_htc,
    fluid_temp,
    wall_htc,
    face_dest,
    face_cell,
    face_count,
):
    layers, cells_x, cells_s = solid_temp.shape
    slots = fluid_temp.shape[0]
    cap = 32
    blocks = slots // LANES
    rows = cells_s + 2 * EDGE
    tall = rows + 2 * PAD
    vmem = pl.BlockSpec(memory_space=pltpu.VMEM)
    hbm = pl.BlockSpec(memory_space=pltpu.HBM)
    big = pltpu.VMEM((tall * 8, LANES), f32)
    faces_f = pltpu.VMEM((blocks, LANES), f32)
    faces_i = pltpu.VMEM((blocks, LANES), jnp.int32)
    faces = pltpu.VMEM((LANES, 1, LANES), f32)
    ext = pltpu.VMEM((layers, LANES, cells_s), f32)
    temp, fluid, flux = pl.pallas_call(
        functools.partial(kernel, n_blade, n_span, cap),
        out_shape=(
            jax.ShapeDtypeStruct(solid_temp.shape, f32),
            jax.ShapeDtypeStruct((blocks, LANES), f32),
            jax.ShapeDtypeStruct((blocks, LANES), f32),
        ),
        in_specs=[hbm] * 7 + [vmem],
        out_specs=(hbm, vmem, vmem),
        scratch_shapes=[
            faces_f,
            faces_f,
            faces_i,
            faces_i,
            ext,
            ext,
            pltpu.VMEM((LANES, cells_s), f32),
            ext,
            pltpu.VMEM((FIELDS * cells_x, 2 * cells_s), f32),
            [big] * 3,
            [big] * 3,
            big,
            big,
            big,
            pltpu.VMEM((rows, LANES), f32),
            pltpu.VMEM((FIELDS, rows, LANES), f32),
            big,
            big,
            pltpu.VMEM((SUBITERS, rows, LANES), f32),
            pltpu.VMEM((LANES, slots), bf16),
            pltpu.VMEM((blocks, LANES), f32),
            faces,
            faces,
            faces,
            faces,
            pltpu.VMEM((cap, LANES), jnp.int32),
            pltpu.VMEM((cap, LANES), jnp.int32),
            pltpu.VMEM((FIELDS, cap, LANES), f32),
            pltpu.VMEM((2 * cells_s, cap * LANES), bf16),
            pltpu.VMEM((SUBITERS * PIECES * cells_x // 2, 2 * cells_s), bf16),
            pltpu.SemaphoreType.DMA((7,)),
            pltpu.SemaphoreType.DMA((24,)),
            pltpu.SemaphoreType.DMA((24,)),
            pltpu.SemaphoreType.DMA((2,)),
            pltpu.SemaphoreType.DMA((2,)),
            pltpu.VMEM((2, SPAN_HALO * 8, LANES), f32),
            pltpu.VMEM((2, EDGE, LANES), f32),
        ],
        compiler_params=pltpu.CompilerParams(
            collective_id=0, has_side_effects=True, vmem_limit_bytes=67043328
        ),
    )(
        solid_temp,
        base_conductivity,
        coolant_htc,
        fluid_temp.reshape(blocks, LANES),
        wall_htc.reshape(blocks, LANES),
        face_dest.reshape(blocks, LANES),
        face_cell.reshape(blocks, LANES),
        face_count.reshape(1, 1),
    )
    return temp, fluid.reshape(slots), flux.reshape(slots)


def solution(mesh):
    placed = (
        P(None, "blade", "span"),
        P(None, "blade", "span"),
        P("blade", "span"),
        P(("blade", "span")),
        P(("blade", "span")),
        P(("blade", "span"), None),
        P(("blade", "span")),
        P(("blade", "span")),
    )
    return jax.shard_map(
        functools.partial(shards, mesh.shape["blade"], mesh.shape["span"]),
        mesh=mesh,
        in_specs=placed,
        out_specs=(P(None, "blade", "span"), P(("blade", "span")), P(("blade", "span"))),
        check_vma=False,
    )
```

```python
import functools

import jax
import jax.numpy as jnp
from jax import lax
from jax.experimental import pallas as pl
from jax.experimental.pallas import tpu as pltpu
from jax.sharding import PartitionSpec as P

SWEEPS = 6
SUBITERS = 4
HALO = SWEEPS * SUBITERS
LANES = 128
FIELDS = 2 * SUBITERS
PIECES = 3
CHUNK = 24
PAD = 24
SPAN_HALO = HALO // 2
EDGE = 16
MESH = pl.DeviceIdType.MESH
f32 = jnp.float32
bf16 = jnp.bfloat16


def iota(shape, dim):
    return lax.broadcasted_iota(jnp.int32, shape, dim)


def split(value, parts):
    pieces = []
    for _ in range(parts):
        piece = value.astype(bf16)
        pieces.append(piece)
        value = value - piece.astype(f32)
    return pieces


def nt(a, b):
    return lax.dot_general(a, b, (((1,), (1,)), ((), ())), preferred_element_type=f32)


def nn(a, b):
    return jnp.dot(a, b, preferred_element_type=f32)


def kernel(
    n_blade,
    n_span,
    cap,
    solid_ref,
    kappa_ref,
    cool_ref,
    fluid_ref,
    htc_ref,
    dest_ref,
    cell_ref,
    count_ref,
    solid_out,
    fluid_out,
    flux_out,
    fluid,
    htc,
    dest,
    cells,
    ext_t,
    ext_k,
    ext_c,
    ext_f,
    acc,
    state_a,
    state_b,
    rho,
    rho_up,
    rho_down,
    cool,
    fields,
    numer_add,
    denom_add,
    tw,
    owner,
    rank,
    send_fwd,
    recv_fwd,
    send_back,
    recv_back,
    slot_x,
    slot_s,
    slot_v,
    pick,
    wall,
    local_sem,
    halo_send,
    halo_recv,
    face_send,
    face_recv,
    landing,
    landing_tw,
):
    devices = n_blade * n_span
    layers, cells_x, cells_s = solid_ref.shape
    blocks = fluid_ref.shape[0]
    temp_a = state_a[0]
    ib, js = lax.axis_index("blade"), lax.axis_index("span")
    me = ib * n_span + js
    lo, hi = HALO, HALO + cells_x
    s_lo, s_hi = EDGE, EDGE + cells_s
    rows = cells_s + 2 * EDGE

    barrier = pltpu.get_barrier_semaphore()

    loads = [
        pltpu.make_async_copy(src, dst, local_sem.at[i])
        for i, (src, dst) in enumerate(
            (
                (dest_ref, dest),
                (cell_ref, cells),
                (htc_ref, htc),
                (fluid_ref, fluid),
                (solid_ref, ext_t.at[:, lo:hi, :]),
                (kappa_ref, ext_k.at[:, lo:hi, :]),
                (cool_ref, ext_c.at[lo:hi, :]),
            )
        )
    ]
    for load in loads:
        load.start()

    def peers(visit):
        unit = 7 if (devices - 1) % 7 == 1 else 1
        if unit > 1:
            visit_one(visit, devices - 1)

        @pl.loop(0, (devices - 1) // unit)
        def _(i):
            for j in range(unit):
                visit_one(visit, i * unit + j + 1)

    def visit_one(visit, k):
        peer = lax.rem(me + k, devices)
        visit(peer, (lax.div(peer, n_span), lax.rem(peer, n_span)))

    peers(
        lambda _, at: pl.semaphore_signal(barrier, inc=1, device_id=at, device_id_type=MESH)
    )
    for load in loads[:4]:
        load.wait()

    number = iota((blocks, LANES), 0) * LANES + iota((blocks, LANES), 1)
    live = number < jnp.broadcast_to(count_ref[...], (blocks, LANES))
    owner_row = jnp.where(live, dest[...], -1)
    before = (iota((LANES, 2 * LANES), 0) < iota((LANES, 2 * LANES), 1)) | (
        iota((LANES, 2 * LANES), 1) >= LANES
    )
    before = before.astype(f32).astype(bf16)
    dev_iota = iota((LANES, LANES), 0)
    offset = jnp.zeros((LANES, LANES), f32)
    packed = jnp.zeros((LANES, LANES), f32)
    cell_f = cells[...].astype(f32)
    slot_iota = iota((cap, LANES), 0).astype(f32)
    for b in range(blocks):
        mine = jnp.where(dev_iota == owner_row[b : b + 1, :], 1.0, 0.0)
        mine_b = mine.astype(bf16)
        owner[:, b * LANES : (b + 1) * LANES] = mine_b
        counts = nn(mine_b, before)
        order = jnp.sum(mine * (counts[:, :LANES] + offset), axis=0, keepdims=True)
        offset = offset + counts[:, LANES:]
        rank[b : b + 1, :] = order
        at_slot = slot_iota == order
        spread = jnp.concatenate(
            [
                jnp.where(at_slot, row[b : b + 1, :], 0.0)
                for row in (htc[...], fluid[...], cell_f)
            ]
            + [jnp.zeros((LANES - 3 * cap, LANES), f32)],
            axis=0,
        )
        for piece in split(spread, 3):
            packed = packed + nt(mine_b, piece)
    send_fwd[...] = packed.reshape(LANES, 1, LANES)
    if devices < LANES:
        recv_fwd[...] = jnp.zeros_like(recv_fwd)
        recv_back[...] = jnp.zeros_like(recv_back)

    pl.semaphore_wait(barrier, devices - 1)

    west = (lax.rem(ib + n_blade - 1, n_blade), js)
    east = (lax.rem(ib + 1, n_blade), js)
    south = (ib, lax.rem(js + n_span - 1, n_span))
    north = (ib, lax.rem(js + 1, n_span))

    def remote(src, dst, sem, to):
        return pltpu.make_async_remote_copy(
            src_ref=src,
            dst_ref=dst,
            send_sem=halo_send.at[sem],
            recv_sem=halo_recv.at[sem],
            device_id=to,
            device_id_type=MESH,
        )

    def across_blade(src, first, last, ext, sem):
        return (
            remote(src.at[..., first : first + HALO, :], ext.at[..., hi : hi + HALO, :], sem, west),
            remote(src.at[..., last - HALO : last, :], ext.at[..., 0:HALO, :], sem + 1, east),
        )

    x_halos = (
        across_blade(solid_ref, 0, cells_x, ext_t, 0)
        + across_blade(kappa_ref, 0, cells_x, ext_k, 2)
        + across_blade(cool_ref, 0, cells_x, ext_c, 4)
    )
    for copy in x_halos:
        copy.start()

    def exchange(send, recv, which):
        peers(
            lambda peer, at: pltpu.make_async_remote_copy(
                src_ref=send.at[peer],
                dst_ref=recv.at[me],
                send_sem=face_send.at[which],
                recv_sem=face_recv.at[which],
                device_id=at,
                device_id_type=MESH,
            ).start()
        )

        recv[pl.ds(me, 1)] = send[pl.ds(me, 1)]

    def arrived(send, recv, which):
        whole = pltpu.make_async_remote_copy(
            src_ref=send.at[pl.ds(0, devices - 1)],
            dst_ref=recv.at[pl.ds(0, devices - 1)],
            send_sem=face_send.at[which],
            recv_sem=face_recv.at[which],
            device_id=east,
            device_id_type=MESH,
        )
        whole.wait_send()
        whole.wait_recv()

    exchange(send_fwd, recv_fwd, 0)

    numer_add[...] = jnp.zeros_like(numer_add)
    denom_add[...] = jnp.zeros_like(denom_add)
    for load in loads[4:]:
        load.wait()
    for copy in x_halos:
        copy.wait()
    for l in range(layers):
        column = pl.ds((PAD + s_lo) * 8 + l, cells_s, stride=8)
        temp_a[column, :] = 0.5 * ext_t[l].T
        rho[column, :] = 1.0 / ext_k[l].T
    cool[s_lo:s_hi, :] = ext_c[...].T

    def across_span(ref, unit, pad, count, sem, land=None):
        first, last = (pad + s_lo) * unit, (pad + s_hi) * unit
        width = count * unit

        def part(start):
            if len(ref.shape) == 3:
                return ref.at[:, start : start + width, :]
            return ref.at[start : start + width, :]

        above, below = (part(last), part(first - width)) if land is None else land
        return (
            remote(part(first), above, sem, south),
            remote(part(last - width), below, sem + 1, north),
        )

    s_halos = (
        across_span(temp_a, 8, PAD, SPAN_HALO, 6)
        + across_span(rho, 8, PAD, SPAN_HALO, 8)
        + across_span(cool, 1, 0, EDGE, 10)
    )
    for copy in s_halos:
        copy.start()

    arrived(send_fwd, recv_fwd, 0)
    got = recv_fwd[...].reshape(LANES, LANES).T
    h = got[0:cap]
    tf = got[cap : 2 * cap]
    cell = got[2 * cap : 3 * cap].astype(jnp.int32)
    x_cell = cell // cells_s
    slot_x[...] = x_cell // 2
    slot_s[...] = cell - (x_cell // 2) * (2 * cells_s)
    inv = 1.0 / (h + 2.0)
    keep = 2.0 * inv
    value = 0.5 * h
    slot_v[0] = value
    value = 0.25 * h * tf
    for n in range(SUBITERS):
        slot_v[1 + n] = value
        value = value * keep
    value = 0.5 * h * (h * inv)
    for n in range(SUBITERS - 1):
        slot_v[1 + SUBITERS + n] = value
        value = value * keep
    acc[...] = jnp.zeros_like(acc)
    half = cells_x // 2
    x_iota = iota((half, LANES), 0)
    s_iota = iota((2 * cells_s, LANES), 0)
    group = 8

    def scatter(fresh, chosen):
        span = 2 * len(chosen) * half
        base = 2 * chosen[0] * half

        @pl.loop(0, cap // group)
        def _(g):
            lhs, rhs = [], []
            for j in range(group):
                r = g * group + j
                row = pl.ds(r, 1)
                lanes = pl.ds(pl.multiple_of(r * LANES, LANES), LANES)
                if fresh:
                    s_hit = jnp.where(s_iota == slot_s[row, :], 1.0, 0.0).astype(bf16)
                    pick[:, lanes] = s_hit
                else:
                    s_hit = pick[:, lanes]
                x_hit = x_iota == slot_x[row, :]
                upper, lower = [], []
                for k in chosen:
                    v = slot_v[k, row, :]
                    v_up = v.astype(bf16).astype(f32)
                    upper.append(jnp.where(x_hit, v_up, 0.0).astype(bf16))
                    lower.append(jnp.where(x_hit, v - v_up, 0.0).astype(bf16))
                lhs.append(jnp.concatenate(upper + lower, axis=0))
                rhs.append(s_hit)
            acc[base : base + span, :] += nt(
                jnp.concatenate(lhs, axis=1), jnp.concatenate(rhs, axis=1)
            )

        for i, k in enumerate(chosen):
            for odd in range(2):
                lanes = slice(odd * cells_s, (odd + 1) * cells_s)
                up = base + i * half
                low = up + len(chosen) * half
                ext_f[k, pl.ds(lo + odd, half, stride=2), :] = (
                    acc[up : up + half, lanes] + acc[low : low + half, lanes]
                )

    def turn(chosen):
        for k in chosen:
            fields[k, s_lo:s_hi, :] = ext_f[k].T

    soon, later = range(0, 2), range(2, FIELDS)
    ext_soon, ext_later = ext_f.at[0:2], ext_f.at[2:FIELDS]
    scatter(True, soon)
    f_x = across_blade(ext_soon, lo, hi, ext_soon, 12)
    for copy in f_x:
        copy.start()
    scatter(False, later)
    late_x = across_blade(ext_later, lo, hi, ext_later, 18)
    for copy in late_x:
        copy.start()

    lane = iota((8, LANES), 1)
    inside_x = ((lane >= lo) | (ib > 0)) & ((lane < hi) | (ib < n_blade - 1))

    def tile(s):
        return pl.ds(pl.multiple_of((s + PAD) * 8, 8), 8)

    def sides(s, to, count=CHUNK):
        for j in range(count):
            at = tile(s + j)
            t = to[0][at, :]
            to[1][at, :] = pltpu.roll(t, LANES - 1, 1)
            to[2][at, :] = pltpu.roll(t, 1, 1)

    def fill(i):
        inside = inside_x & (
            ((i >= s_lo // 8) | (js > 0)) & ((i < s_hi // 8) | (js < n_span - 1))
        )
        for j in range(8):
            at = tile(i * 8 + j)
            held = jnp.where(inside, rho[at, :], 1e15)
            rho[at, :] = held
            rho_up[at, :] = pltpu.roll(held, LANES - 1, 1)
            rho_down[at, :] = pltpu.roll(held, 1, 1)
        sides(i * 8, state_a, 8)

    edge = EDGE // 8

    @pl.loop(2 * edge, rows // 8 - 2 * edge)
    def _(i):
        fill(i)

    for copy in f_x:
        copy.wait()
    turn(soon)
    f_s = across_span(fields.at[0:2], 1, 0, EDGE, 14)
    for copy in f_s:
        copy.start()
    for copy in s_halos:
        copy.wait()

    @pl.loop(0, 2 * edge)
    def _(i):
        fill(i)
        fill(i + rows // 8 - 2 * edge)

    for copy in late_x:
        copy.wait()
    turn(later)
    late_s = across_span(fields.at[2:FIELDS], 1, 0, EDGE, 20)
    for copy in late_s:
        copy.start()
    for copy in f_s:
        copy.wait()

    every = pl.ds(PAD * 8, rows, stride=8)
    denom_add[every, :] = fields[0]
    denom_add[pl.ds(PAD * 8 + layers - 1, rows, stride=8), :] = 0.5 * cool[...]
    not_last = jnp.where(iota((8, LANES), 0) < layers - 1, 1.0, 0.0)

    def chunks(first):
        return (rows - 2 * first + CHUNK - 1) // CHUNK

    def last_chunk(first):
        return first + (chunks(first) - 1) * CHUNK

    def sweep(src, dst, step):
        first = EDGE - SPAN_HALO + 1 + step

        def chunk(i, carry, done=None):
            t_prev, t_here, r_here, w_prev = carry
            start = first + i * CHUNK
            if done is None:
                sides(start - CHUNK, dst)
            for j in range(CHUNK):
                at, after = tile(start + j), tile(start + j + 1)
                t_next = src[0][after, :]
                r_next = resist(t_next, rho[after, :])
                t_up, t_down = src[1][at, :], src[2][at, :]
                w_next = 1.0 / (r_here + r_next)
                w_up = 1.0 / (r_here + resist(t_up, rho_up[at, :]))
                w_down = 1.0 / (r_here + resist(t_down, rho_down[at, :]))
                w_in = not_last / (r_here + pltpu.roll(r_here, 7, 0))
                w_out = pltpu.roll(w_in, 1, 0)
                numer = (
                    (w_next * t_next + w_prev * t_prev)
                    + (w_up * t_up + w_down * t_down)
                    + (w_in * pltpu.roll(t_here, 7, 0) + w_out * pltpu.roll(t_here, 1, 0))
                    + numer_add[at, :]
                )
                denom = ((w_next + w_prev) + (w_up + w_down)) + (
                    (w_in + w_out) + denom_add[at, :]
                )
                dst[0][at, :] = numer / denom
                t_prev, t_here, r_here, w_prev = t_here, t_next, r_next, w_next
            if done is not None:
                sides(done, src)
            return t_prev, t_here, r_here, w_prev

        def resist(t, held):
            return held / (1.0 + t * t)

        before, here = tile(first - 1), tile(first)
        t_prev, t_here = src[0][before, :], src[0][here, :]
        r_here = resist(t_here, rho[here, :])
        w_prev = 1.0 / (resist(t_prev, rho[before, :]) + r_here)
        carry = chunk(0, (t_prev, t_here, r_here, w_prev), last_chunk(first - 1))
        lax.fori_loop(1, chunks(first), chunk, carry)

    def find(early):
        pair = 2 * PIECES * half

        @pl.loop(0, cap // 8)
        def _(g):
            width = 8 * LANES
            lanes = pl.ds(pl.multiple_of(g * width, width), width)
            found = nn(wall[early * PIECES * half : early * PIECES * half + pair, :], pick[:, lanes])
            for j in range(8):
                row = pl.ds(g * 8 + j, 1)
                x_hit = x_iota == slot_x[row, :]
                for n in range(2):
                    at = n * PIECES * half
                    total = found[at : at + half, j * LANES : (j + 1) * LANES]
                    for p in range(1, PIECES):
                        total = total + found[
                            at + p * half : at + (p + 1) * half, j * LANES : (j + 1) * LANES
                        ]
                    slot_v[early + n, row, :] = jnp.sum(
                        jnp.where(x_hit, total, 0.0), axis=0, keepdims=True
                    )

    for n in range(SUBITERS):
        if n == 1:
            for copy in late_s:
                copy.wait()
        extra = fields[1 + n]
        for m in range(n):
            extra = extra + tw[m] * fields[SUBITERS + n - m]
        numer_add[every, :] = extra

        @pl.loop(0, SWEEPS // 2)
        def _(p):
            step = n % 2 * SWEEPS + 2 * p
            sweep(state_a, state_b, step)
            sweep(state_b, state_a, step + 1)

        now = temp_a[every, :]
        tw[n] = now
        ext_c[...] = now[s_lo:s_hi, :].T
        for odd in range(2):
            pieces = split(ext_c[pl.ds(lo + odd, half, stride=2), :], PIECES)
            for p, piece in enumerate(pieces):
                at = (n * PIECES + p) * half
                wall[at : at + half, odd * cells_s : (odd + 1) * cells_s] = piece
        if n == 1:
            middle = across_span(
                temp_a, 8, PAD, SPAN_HALO, 16, (landing.at[1], landing.at[0])
            ) + across_span(
                tw.at[0], 1, 0, EDGE, 22, (landing_tw.at[1], landing_tw.at[0])
            )
            for copy in middle:
                copy.start()
            find(0)
            sides(last_chunk(s_lo), state_a)
            for copy in middle:
                copy.wait()
            for side, start in enumerate((s_lo - SPAN_HALO, s_hi)):
                at = (start + PAD) * 8
                temp_a[at : at + SPAN_HALO * 8, :] = landing[side]
                sides(start, state_a, SPAN_HALO)
                tw[0, side * s_hi : side * s_hi + EDGE, :] = landing_tw[side]
            tw[1] = temp_a[every, :]
    find(2)

    got = recv_fwd[...].reshape(LANES, LANES).T
    h = got[0:cap]
    tf = got[cap : 2 * cap]
    inv = 1.0 / (h + 2.0)
    for n in range(SUBITERS):
        q = h * (tf - 2.0 * slot_v[n])
        tf = tf - q * inv
    back = jnp.concatenate([q, tf, jnp.zeros((LANES - 2 * cap, LANES), f32)], axis=0)
    send_back[...] = back.T.reshape(LANES, 1, LANES)
    exchange(send_back, recv_back, 1)

    for l in range(layers):
        final = temp_a[pl.ds((PAD + s_lo) * 8 + l, cells_s, stride=8), :]
        ext_k[l, 0:cells_x, :] = 2.0 * final.T[lo:hi, :]
    store = pltpu.make_async_copy(ext_k.at[:, 0:cells_x, :], solid_out, local_sem.at[0])
    store.start()

    arrived(send_back, recv_back, 1)
    table = recv_back[...].reshape(LANES, LANES).T[0 : 2 * cap]
    pieces = jnp.concatenate(split(table, 3), axis=0)
    for b in range(blocks):
        seen = nn(pieces, owner[:, b * LANES : (b + 1) * LANES])
        seen = seen[0 : 2 * cap] + seen[2 * cap : 4 * cap] + seen[4 * cap : 6 * cap]
        at_slot = slot_iota == rank[b : b + 1, :]
        q_row = jnp.sum(jnp.where(at_slot, seen[0:cap], 0.0), axis=0, keepdims=True)
        t_row = jnp.sum(jnp.where(at_slot, seen[cap : 2 * cap], 0.0), axis=0, keepdims=True)
        on = live[b : b + 1, :]
        flux_out[b : b + 1, :] = jnp.where(on, q_row, 0.0)
        fluid_out[b : b + 1, :] = jnp.where(on, t_row, fluid[b : b + 1, :])
    store.wait()


def shards(
    n_blade,
    n_span,
    solid_temp,
    base_conductivity,
    coolant_htc,
    fluid_temp,
    wall_htc,
    face_dest,
    face_cell,
    face_count,
):
    layers, cells_x, cells_s = solid_temp.shape
    slots = fluid_temp.shape[0]
    cap = 32
    blocks = slots // LANES
    rows = cells_s + 2 * EDGE
    tall = rows + 2 * PAD
    vmem = pl.BlockSpec(memory_space=pltpu.VMEM)
    hbm = pl.BlockSpec(memory_space=pltpu.HBM)
    big = pltpu.VMEM((tall * 8, LANES), f32)
    faces_f = pltpu.VMEM((blocks, LANES), f32)
    faces_i = pltpu.VMEM((blocks, LANES), jnp.int32)
    faces = pltpu.VMEM((LANES, 1, LANES), f32)
    ext = pltpu.VMEM((layers, LANES, cells_s), f32)
    temp, fluid, flux = pl.pallas_call(
        functools.partial(kernel, n_blade, n_span, cap),
        out_shape=(
            jax.ShapeDtypeStruct(solid_temp.shape, f32),
            jax.ShapeDtypeStruct((blocks, LANES), f32),
            jax.ShapeDtypeStruct((blocks, LANES), f32),
        ),
        in_specs=[hbm] * 7 + [vmem],
        out_specs=(hbm, vmem, vmem),
        scratch_shapes=[
            faces_f,
            faces_f,
            faces_i,
            faces_i,
            ext,
            ext,
            pltpu.VMEM((LANES, cells_s), f32),
            ext,
            pltpu.VMEM((FIELDS * cells_x, 2 * cells_s), f32),
            [big] * 3,
            [big] * 3,
            big,
            big,
            big,
            pltpu.VMEM((rows, LANES), f32),
            pltpu.VMEM((FIELDS, rows, LANES), f32),
            big,
            big,
            pltpu.VMEM((SUBITERS, rows, LANES), f32),
            pltpu.VMEM((LANES, slots), bf16),
            pltpu.VMEM((blocks, LANES), f32),
            faces,
            faces,
            faces,
            faces,
            pltpu.VMEM((cap, LANES), jnp.int32),
            pltpu.VMEM((cap, LANES), jnp.int32),
            pltpu.VMEM((FIELDS, cap, LANES), f32),
            pltpu.VMEM((2 * cells_s, cap * LANES), bf16),
            pltpu.VMEM((SUBITERS * PIECES * cells_x // 2, 2 * cells_s), bf16),
            pltpu.SemaphoreType.DMA((7,)),
            pltpu.SemaphoreType.DMA((24,)),
            pltpu.SemaphoreType.DMA((24,)),
            pltpu.SemaphoreType.DMA((2,)),
            pltpu.SemaphoreType.DMA((2,)),
            pltpu.VMEM((2, SPAN_HALO * 8, LANES), f32),
            pltpu.VMEM((2, EDGE, LANES), f32),
        ],
        compiler_params=pltpu.CompilerParams(
            collective_id=0, has_side_effects=True, vmem_limit_bytes=67043328
        ),
    )(
        solid_temp,
        base_conductivity,
        coolant_htc,
        fluid_temp.reshape(blocks, LANES),
        wall_htc.reshape(blocks, LANES),
        face_dest.reshape(blocks, LANES),
        face_cell.reshape(blocks, LANES),
        face_count.reshape(1, 1),
    )
    return temp, fluid.reshape(slots), flux.reshape(slots)


def solution(mesh):
    placed = (
        P(None, "blade", "span"),
        P(None, "blade", "span"),
        P("blade", "span"),
        P(("blade", "span")),
        P(("blade", "span")),
        P(("blade", "span"), None),
        P(("blade", "span")),
        P(("blade", "span")),
    )
    return jax.shard_map(
        functools.partial(shards, mesh.shape["blade"], mesh.shape["span"]),
        mesh=mesh,
        in_specs=placed,
        out_specs=(P(None, "blade", "span"), P(("blade", "span")), P(("blade", "span"))),
        check_vma=False,
    )
```
